512 devices in a mesh: dp: 64 (over z_lo, x, core), expert: 8 (over z_hi, y).
Axes of the slice: x: 4, y: 4, z: 16 (z_hi: 2, z_lo: 8; z = z_hi * 8 + z_lo), core: 2. Of those that a mesh axis runs over, the one named last changes fastest.
Arguments:
- tokens: bfloat16 [768, 2048], P('dp', 'expert'), may hold values from -6 to 6
- cotangent: bfloat16 [768, 2048], P('dp', 'expert'), may hold values from -6 to 6
- route: int32 [768, 2], P('dp'), may hold values from 0 to 7, all different within a row; in each aligned block of 12 rows (0 to 11, 12 to 23, ...) at most 4 rows name the same one
- gates: float32 [768, 2], P('dp'), may hold values from 0.25 to 1
- w_gate: bfloat16 [8, 12288, 2048], P('expert', 'dp'), may hold values from -0.125 to 0.125
- w_up: bfloat16 [8, 12288, 2048], P('expert', 'dp'), may hold values from -0.125 to 0.125
- w_down: bfloat16 [8, 12288, 2048], P('expert', 'dp'), may hold values from -0.0546875 to 0.0546875
Outputs:
- mixed: bfloat16 [768, 2048], P('dp', 'expert')
- grad_tokens: bfloat16 [768, 2048], P('dp', 'expert')
- grad_gate: bfloat16 [8, 12288, 2048], P('expert', 'dp')
- grad_up: bfloat16 [8, 12288, 2048], P('expert', 'dp')
- grad_down: bfloat16 [8, 12288, 2048], P('expert', 'dp')
The draws below stay inside these ranges and needn't reach their ends.
Inputs may be any that keep to these rules, and one draw needn't show every extreme that they name: `route`: the two experts of a token differ. Among the 12 tokens of one index of dp, at most 4 name the same expert, and in some such block one expert is named by exactly 4 tokens. Every expert is named by some token.
All inputs are finite; a program needn't handle non-finite values.
Results may differ from the reference program's by a relative error of at most 0.0065.
Values may be sent and summed in bfloat16 or wider, within the bound.
A program may use at most 64 MiB of HBM per device.

```python
import math
import jax
import jax.numpy as jnp
import numpy as np
from jax import lax

D = 2048
F = 12288
TOP = 2
TOK_DEV = 12
EXPERTS = 8
CAP = 4
TOKENS = 768
N_DP = 64


def steps_of(stream_key, extent, split, least, top_value):
    level = 1.0
    for position, blocks in split:
        draws = jax.random.uniform(jax.random.fold_in(jax.random.fold_in(stream_key, 6), position), (blocks,), jnp.float32, least / len(split), top_value / len(split))
        level = level * jnp.repeat(jnp.exp(draws), extent[position] // blocks).reshape((-1,) + (1,) * (len(extent) - 1 - position))
    return level


def assign_block(rng, own, number, rows, number_of, top, bound, lean):
    ranking = jax.random.permutation(rng, number_of)
    packed, usual = portions_of(number_of, rows * top, bound, lean, True), portions_of(number_of, rows * top, bound, lean, False)
    places = jnp.arange(number_of)

    def named(sizes, offset_by):
        used = int((sizes > 0).sum())
        fixed = max(1, used // 4)
        passed = fixed + (places - fixed + offset_by * (used - fixed)) % max(1, number_of - fixed)
        return jnp.zeros((number_of,), jnp.int32).at[ranking[jnp.where(places < fixed, places, passed)]].set(jnp.asarray(sizes, jnp.int32))

    sizes = jnp.where(number % 4 == 0, named(packed, number // 4), named(usual, number - number // 4 - 1))
    mixed = jax.random.permutation(jax.random.fold_in(own, 3), number_of)
    giver, taker = mixed[0:number_of // 2 * 2:2], mixed[1:number_of // 2 * 2:2]
    room = jnp.minimum(sizes[giver] - 1, bound - sizes[taker]) // 2
    room = jnp.where((giver == ranking[0]) | (taker == ranking[0]) | (sizes[taker] == 0), 0, jnp.maximum(room, 0))
    passed = jax.random.randint(jax.random.fold_in(own, 4), (number_of // 2,), 0, 1 << 20) % (room + 1)
    sizes = sizes.at[giver].add(-passed).at[taker].add(passed)
    labels = jnp.searchsorted(jnp.cumsum(sizes), jnp.arange(rows * top), side="right").astype(jnp.int32)
    table = labels.reshape(top, rows).T
    table = table[jax.random.permutation(jax.random.fold_in(own, 1), rows)]
    offset_by = jax.random.randint(jax.random.fold_in(own, 2), (rows, 1), 0, top)
    return jnp.take_along_axis(table, (jnp.arange(top)[None, :] + offset_by) % top, axis=1)


def portions_of(number_of, total, limit, lean, full):
    portions = [(1 << 20) // math.isqrt(grade ** lean) + 1 for grade in range(1, number_of + 1)]
    largest = limit if full else min(limit, max(-(-total // number_of), total * portions[0] // sum(portions)))
    least = 1 if total - largest >= number_of - 1 else 0
    given, rest = [largest] + [least] * (number_of - 1), total - largest - least * (number_of - 1)
    while rest > 0:
        movable = [i for i in range(1, number_of) if given[i] < largest] or [i for i in range(1, number_of) if given[i] < limit]
        whole, remaining = sum([portions[i] for i in movable]), rest
        for i in movable:
            addition = min(limit - given[i], max(1, remaining * portions[i] // whole), rest)
            given[i] = given[i] + addition
            rest = rest - addition
    return np.array(given)


def scatter_about(own_key, shape, spread, bound, split=(), kind=jnp.bfloat16):
    entries = spread * jax.random.normal(own_key, shape, jnp.float32)
    if split:
        entries = entries * steps_of(own_key, shape, split, -0.22, 0.18)
    return jnp.clip(entries, -bound, bound).astype(kind)


def setup_inputs(seed: int = 0) -> dict:
    arg_keys = jax.random.split(jax.random.key(seed), 8)
    tokens = scatter_about(arg_keys[0], (TOKENS, D), 1.0, 6.0, ((0, 64), (1, 8)))
    cotangent = scatter_about(arg_keys[1], (TOKENS, D), 1.0, 6.0, ((0, 64), (1, 8)))
    route_keys = jax.random.split(jax.random.fold_in(arg_keys[2], 1), TOKENS // TOK_DEV)
    route_turns = jax.random.permutation(jax.random.fold_in(arg_keys[2], 3), TOKENS // TOK_DEV)
    route = jax.vmap(lambda own, number: assign_block(jax.random.fold_in(arg_keys[2], 2), own, number, TOK_DEV, EXPERTS, TOP, CAP, 2))(route_keys, route_turns).reshape((TOKENS, TOP))
    gates = jnp.clip(0.25 + 0.75 * jax.random.uniform(arg_keys[3], (TOKENS, TOP), jnp.float32) ** steps_of(arg_keys[3], (TOKENS, TOP), ((0, 64),), -0.2, 0.2), 0.25, 1.0)
    w_gate = scatter_about(arg_keys[4], (EXPERTS, F, D), D ** -0.5, 0.125, ((0, 8), (1, 64)))
    w_up = scatter_about(arg_keys[5], (EXPERTS, F, D), D ** -0.5, 0.125, ((0, 8), (1, 64)))
    w_down = scatter_about(arg_keys[6], (EXPERTS, F, D), F ** -0.5, 0.0546875, ((0, 8), (1, 64)))
    return {"tokens": tokens, "cotangent": cotangent, "route": route, "gates": gates, "w_gate": w_gate, "w_up": w_up, "w_down": w_down}


def slots_of(route):
    assign = route.reshape(N_DP, TOP * TOK_DEV)
    order = jnp.arange(TOP * TOK_DEV, dtype=jnp.int32)
    before = order[None, :] < order[:, None]
    same = (assign[:, :, None] == assign[:, None, :]) & before[None]
    slot = jnp.sum(same.astype(jnp.int32), axis=2).astype(jnp.int32)
    return assign, slot


def dispatch(pairs, assign, slot):
    expert_ids = jnp.arange(EXPERTS, dtype=jnp.int32)
    slot_ids = jnp.arange(CAP, dtype=jnp.int32)
    select = ((assign[:, None, None, :] == expert_ids[None, :, None, None])
              & (slot[:, None, None, :] == slot_ids[None, None, :, None])).astype(jnp.float32)
    placed = jnp.einsum('necj,njd->encd', select, pairs.astype(jnp.float32))
    return placed.astype(jnp.bfloat16).reshape(EXPERTS, N_DP * CAP, D)


def contract_rows(left, right):
    return lax.dot_general(left, right, (((0,), (0,)), ((), ())), preferred_element_type=jnp.float32)


def contract_cols(left, right):
    return lax.dot_general(left, right, (((1,), (1,)), ((), ())), preferred_element_type=jnp.float32)


def expert_pass(operands):
    xs, dys, wg, wu, wd = operands
    pre_gate = contract_cols(xs, wg)
    pre_up = contract_cols(xs, wu)
    sig = jax.nn.sigmoid(pre_gate)
    silu = pre_gate * sig
    hidden = (silu * pre_up).astype(jnp.bfloat16)
    expert_out = jnp.dot(hidden, wd, preferred_element_type=jnp.float32).astype(jnp.bfloat16)
    grad_down = contract_rows(hidden, dys).astype(jnp.bfloat16)
    grad_hidden = contract_cols(dys, wd)
    grad_pre_gate = (grad_hidden * pre_up * sig * (1.0 + pre_gate * (1.0 - sig))).astype(jnp.bfloat16)
    grad_pre_up = (grad_hidden * silu).astype(jnp.bfloat16)
    grad_gate = contract_rows(grad_pre_gate, xs).astype(jnp.bfloat16)
    grad_up = contract_rows(grad_pre_up, xs).astype(jnp.bfloat16)
    grad_slots = (jnp.dot(grad_pre_gate, wg, preferred_element_type=jnp.float32)
                  + jnp.dot(grad_pre_up, wu, preferred_element_type=jnp.float32)).astype(jnp.bfloat16)
    return expert_out, grad_slots, grad_gate, grad_up, grad_down


def pick(slot_rows, assign, slot):
    table = slot_rows.reshape(EXPERTS, N_DP, CAP, D)
    blocks = jnp.arange(N_DP, dtype=jnp.int32)[:, None]
    return table[assign, blocks, slot].astype(jnp.float32)


def reference(tokens, cotangent, route, gates, w_gate, w_up, w_down):
    assign, slot = slots_of(route)
    token_pairs = jnp.repeat(tokens.reshape(N_DP, TOK_DEV, D), TOP, axis=1)
    weighted = (gates[:, :, None] * cotangent[:, None, :].astype(jnp.float32)).astype(jnp.bfloat16)
    weighted = weighted.reshape(N_DP, TOP * TOK_DEV, D)
    xs = dispatch(token_pairs, assign, slot)
    dys = dispatch(weighted, assign, slot)
    expert_out, grad_slots, grad_gate, grad_up, grad_down = lax.map(expert_pass, (xs, dys, w_gate, w_up, w_down))
    gate_flat = gates.reshape(N_DP, TOP * TOK_DEV)
    picked = pick(expert_out, assign, slot) * gate_flat[:, :, None]
    mixed = picked.reshape(N_DP, TOK_DEV, TOP, D).sum(axis=2).reshape(TOKENS, D).astype(jnp.bfloat16)
    back = pick(grad_slots, assign, slot)
    grad_tokens = back.reshape(N_DP, TOK_DEV, TOP, D).sum(axis=2).reshape(TOKENS, D).astype(jnp.bfloat16)
    return mixed, grad_tokens, grad_gate, grad_up, grad_down
```

```python
import functools

import jax
import jax.numpy as jnp
from jax import lax
from jax.experimental import pallas as pl
from jax.experimental.pallas import tpu as pltpu
from jax.sharding import PartitionSpec as P

MESH = pl.DeviceIdType.MESH
BF16 = jnp.bfloat16
F32 = jnp.float32
NX = 4
NC = 2
CAP = 4
ROWS = NX * CAP


def dot(left, right):
    return jnp.dot(left, right, preferred_element_type=F32)


def dot_cols(left, right):
    return lax.dot_general(left, right, (((1,), (1,)), ((), ())), preferred_element_type=F32)


def dot_rows(left, right):
    return lax.dot_general(left, right, (((0,), (0,)), ((), ())), preferred_element_type=F32)


def kernel(
    nz,
    ne,
    tok_ref,
    cot_ref,
    route_ref,
    gates_ref,
    wg_hbm,
    wu_hbm,
    wd_hbm,
    mixed_ref,
    gtok_ref,
    gg_hbm,
    gu_hbm,
    gd_hbm,
    snd,
    rcv,
    g,
    wg,
    wu,
    wd,
    acc,
    hid,
    part,
    sib,
    rel,
    full,
    zbuf,
    rz,
    snd2,
    rcv2,
    gg,
    gu,
    gd,
    w_sem,
    o_sem,
    send_sem,
    d_sem,
    z_sem,
    x_sem,
    c_sem,
    rs_sem,
    rz_sem,
    f_sem,
):
    p = lax.axis_index("dp")
    e = lax.axis_index("expert")
    zl = lax.div(p, NX * NC)
    x = lax.rem(lax.div(p, NC), NX)
    c = lax.rem(p, NC)
    right = lax.rem(x + 1, NX)
    left = lax.rem(x + 3, NX)
    opp = lax.rem(x + 2, NX)
    other = 1 - c
    e_half = lax.div(e, 2)
    e_par = lax.rem(e, 2)
    rows = nz * NC * ROWS
    feat = tok_ref.shape[1]
    chunk = 2 * feat
    toks = tok_ref.shape[0]

    def dp_of(z, xx, cc):
        return z * (NX * NC) + xx * NC + cc

    dev_right = (dp_of(zl, right, c), e)
    dev_left = (dp_of(zl, left, c), e)
    dev_sib = (dp_of(zl, x, other), e)
    sent = []

    def send(src, dst, rsem, device):
        copy = pltpu.make_async_remote_copy(
            src_ref=src,
            dst_ref=dst,
            send_sem=send_sem.at[len(sent)],
            recv_sem=rsem,
            device_id=device,
            device_id_type=MESH,
        )
        copy.start()
        sent.append(copy)

    def arrived(dst, rsem):
        pltpu.make_async_remote_copy(
            src_ref=dst,
            dst_ref=dst,
            send_sem=send_sem.at[0],
            recv_sem=rsem,
            device_id=dev_sib,
            device_id_type=MESH,
        ).wait_recv()

    barrier = pltpu.get_barrier_semaphore()

    def greet(dp, ex):
        pl.semaphore_signal(barrier, inc=1, device_id=(dp, ex), device_id_type=MESH)

    to_self = e_half == x
    for i in range(ne):

        @pl.when(jnp.logical_not(jnp.logical_and(to_self, e == i)))
        def _():
            greet(dp_of(zl, e_half, c), jnp.int32(i))

        xs_i, par_i = i // 2, i % 2

        @pl.when(jnp.logical_not(jnp.logical_and(x == xs_i, e == 2 * x + par_i)))
        def _():
            greet(dp_of(zl, jnp.int32(xs_i), c), 2 * x + par_i)

    for k in range(1, nz):
        greet(dp_of(lax.rem(zl + k, nz), x, c), e)
    greet(*dev_right)
    greet(*dev_left)
    greet(*dev_sib)

    loads = []
    for n, (hbm, vmem) in enumerate(((wg_hbm, wg), (wu_hbm, wu), (wd_hbm, wd))):
        for i in range(NX):
            copy = pltpu.make_async_copy(
                hbm.at[0, :, i * chunk : (i + 1) * chunk], vmem.at[i], w_sem.at[n * NX + i]
            )
            copy.start()
            loads.append(copy)

    lane = lax.broadcasted_iota(jnp.int32, (toks, ne * 2 * CAP), 1)
    lane_e = lane >> 3
    first = ((lane >> 2) & 1) == 0
    lane_c = (lane & 3).astype(F32)
    m0 = (route_ref[:, 0:1] == lane_e).astype(F32)
    m1 = (route_ref[:, 1:2] == lane_e).astype(F32)
    earlier = (
        lax.broadcasted_iota(jnp.int32, (toks, toks), 1)
        < lax.broadcasted_iota(jnp.int32, (toks, toks), 0)
    ).astype(F32)
    before = dot(earlier, m0 + m1)
    p0 = jnp.where(before == lane_c, m0, 0.0)
    p1 = jnp.where(before + m0 == lane_c, m1, 0.0)
    p0_out = jnp.where(first, p0, 0.0).astype(BF16)
    p1_out = jnp.where(first, p1, 0.0).astype(BF16)
    p0_grad = jnp.where(first, 0.0, p0).astype(BF16)
    p1_grad = jnp.where(first, 0.0, p1).astype(BF16)
    cot = cot_ref[...].astype(F32)
    weighted0 = (gates_ref[:, 0:1] * cot).astype(BF16)
    weighted1 = (gates_ref[:, 1:2] * cot).astype(BF16)
    placed = (
        dot_rows(p0_out + p1_out, tok_ref[...])
        + dot_rows(p0_grad, weighted0)
        + dot_rows(p1_grad, weighted1)
    )
    snd[...] = placed.reshape(ne, 2 * CAP, feat)

    pl.semaphore_wait(barrier, jnp.where(to_self, 2 * ne - 2, 2 * ne) + (nz - 1) + 3)

    def dispatch_copy(i):
        return pltpu.make_async_remote_copy(
            src_ref=snd.at[i],
            dst_ref=rcv.at[x * 2 + e_par],
            send_sem=d_sem.at[0, i],
            recv_sem=d_sem.at[1, x * 2 + e_par],
            device_id=(dp_of(zl, e_half, c), jnp.int32(i)),
            device_id_type=MESH,
        )

    for i in range(ne):
        mine = jnp.logical_and(to_self, e == i)

        @pl.when(mine)
        def _():
            rcv[x * 2 + e_par] = snd[i]

        @pl.when(jnp.logical_not(mine))
        def _():
            dispatch_copy(i).start()

    for i in range(ne):

        @pl.when(jnp.logical_not(jnp.logical_and(x == i // 2, e == 2 * x + i % 2)))
        def _():
            arrived(rcv.at[i], d_sem.at[1, i])

    sub = lax.broadcasted_iota(jnp.int32, (8, feat), 0) < CAP
    for par in range(2):
        t = [rcv[2 * i + par] for i in range(NX)]
        r = [pltpu.roll(v, CAP, 0) for v in t]
        cols = slice(par * feat, (par + 1) * feat)
        xs_rows = [jnp.where(sub, t[0], r[1]), jnp.where(sub, t[2], r[3])]
        dy_rows = [jnp.where(sub, r[0], t[1]), jnp.where(sub, r[2], t[3])]
        g[0, x, c, zl, :, cols] = jnp.concatenate(xs_rows, axis=0).astype(BF16)
        g[1, x, c, zl, :, cols] = jnp.concatenate(dy_rows, axis=0).astype(BF16)

    for k in range(1, nz):
        far = lax.rem(zl + k, nz)
        send(g.at[:, x, c, zl], g.at[:, x, c, zl], z_sem.at[zl], (dp_of(far, x, c), e))

    h = lax.div(zl, 2)
    pairs = [h, h + 1 - 2 * lax.rem(h, 2), lax.rem(h + 2, 4), 3 - h]

    def region(xi, cc, k):
        return g.at[:, xi, cc, pl.ds(2 * pairs[k], 2)]

    def half(a, xi, k):
        return g.at[a, xi, c, pl.ds(2 * pairs[k], 2)]

    def stage_a(k):
        if k == 0:
            z = zl + 1 - 2 * lax.rem(zl, 2)
            arrived(g.at[:, x, c, z], z_sem.at[z])
        else:
            for j in range(2):
                z = 2 * pairs[k] + j
                arrived(g.at[:, x, c, z], z_sem.at[z])
        send(region(x, c, k), region(x, c, k), x_sem.at[0, k], dev_right)
        send(region(x, c, k), region(x, c, k), x_sem.at[1, k], dev_left)
        send(region(x, c, k), region(x, c, k), c_sem.at[0, k], dev_sib)

    def stage_b(k):
        arrived(region(left, c, k), x_sem.at[0, k])
        send(half(0, left, k), half(0, left, k), x_sem.at[2, k], dev_right)
        send(region(left, c, k), region(left, c, k), c_sem.at[1, k], dev_sib)
        arrived(region(right, c, k), x_sem.at[1, k])
        send(half(1, right, k), half(1, right, k), x_sem.at[3, k], dev_left)
        send(region(right, c, k), region(right, c, k), c_sem.at[2, k], dev_sib)

    def stage_c(k):
        arrived(half(0, opp, k), x_sem.at[2, k])
        arrived(half(1, opp, k), x_sem.at[3, k])
        send(region(opp, c, k), region(opp, c, k), c_sem.at[3, k], dev_sib)

    for copy in loads:
        copy.wait()
    ng = nz // 2
    for k in range(ng + 2):
        if k < ng:
            stage_a(k)
        if 0 <= k - 1 < ng:
            stage_b(k - 1)
        if 0 <= k - 2 < ng:
            stage_c(k - 2)

    for n, xi in enumerate((x, left, right, opp)):
        for k in range(ng):
            arrived(region(xi, other, k), c_sem.at[n, k])
        xs = g[0, xi].reshape(rows, chunk)
        dys = g[1, xi].reshape(rows, chunk)
        terms = (dot_cols(xs, wg[xi]), dot_cols(xs, wu[xi]), dot_cols(dys, wd[xi]))
        for i in range(3):
            acc[i] = terms[i] if n == 0 else acc[i] + terms[i]

    pre_gate = acc[0]
    pre_up = acc[1]
    grad_hidden = acc[2]
    sig = jax.nn.sigmoid(pre_gate)
    silu = pre_gate * sig
    hid[0] = (silu * pre_up).astype(BF16)
    hid[1] = (grad_hidden * pre_up * sig * (1.0 + pre_gate * (1.0 - sig))).astype(BF16)
    hid[2] = (grad_hidden * silu).astype(BF16)

    for n, xi in enumerate((opp, right, left, x)):
        y0 = dot(hid[0], wd[xi])
        y1 = dot(hid[1], wg[xi]) + dot(hid[2], wu[xi])
        part[0, xi] = y0.astype(BF16).reshape(NC, nz, ROWS, chunk)
        part[1, xi] = y1.astype(BF16).reshape(NC, nz, ROWS, chunk)
        send(part.at[:, xi, other], sib.at[:, xi], rs_sem.at[n], dev_sib)

    def chip_sum(n, a, xi):
        return part[a, xi, c].astype(F32) + sib[a, xi].astype(F32)

    arrived(sib.at[:, opp], rs_sem.at[0])
    for a in range(2):
        part[a, opp, c] = chip_sum(0, a, opp).astype(BF16)
        send(part.at[a, opp, c], rel.at[a], rs_sem.at[4 + a], (dev_right, dev_left)[a])

    def weight_grad(n, left_rows, a, out, hbm):
        for i in range(NX):
            out[i] = dot_rows(left_rows, g[a, i].reshape(rows, chunk)).astype(BF16)
            copy = pltpu.make_async_copy(
                out.at[i], hbm.at[0, :, i * chunk : (i + 1) * chunk], o_sem.at[n * NX + i]
            )
            copy.start()
            loads.append(copy)

    del loads[:]
    weight_grad(0, hid[0], 1, gd, gd_hbm)

    for n, xi, device in ((0, right, dev_right), (1, left, dev_left)):
        arrived(sib.at[:, xi], rs_sem.at[1 + n])
        part[1 - n, xi, c] = chip_sum(1 + n, 1 - n, xi).astype(BF16)
        arrived(rel.at[n], rs_sem.at[4 + n])
        part[n, xi, c] = (chip_sum(1 + n, n, xi) + rel[n].astype(F32)).astype(BF16)
        send(part.at[:, xi, c], full.at[n], rs_sem.at[6 + n], device)

    weight_grad(1, hid[1], 0, gg, gg_hbm)
    weight_grad(2, hid[2], 0, gu, gu_hbm)

    arrived(sib.at[:, x], rs_sem.at[3])
    arrived(full.at[0], rs_sem.at[6])
    arrived(full.at[1], rs_sem.at[7])
    for a in range(2):
        total = chip_sum(3, a, x) + full[0, a].astype(F32) + full[1, a].astype(F32)
        zbuf[:, a] = total.astype(BF16)
    for k in range(1, nz):
        far = lax.rem(zl + k, nz)
        send(zbuf.at[far], rz.at[zl], rz_sem.at[zl], (dp_of(far, x, c), e))
    total = zbuf[zl].astype(F32)
    for k in range(1, nz):
        far = lax.rem(zl + k, nz)
        arrived(rz.at[far], rz_sem.at[far])
        total = total + rz[far].astype(F32)
    total = total.astype(BF16).astype(F32)

    for par in range(2):
        cols = slice(par * feat, (par + 1) * feat)
        for i in range(2):
            out_rows = total[0, 8 * i : 8 * i + 8, cols]
            grad_rows = total[1, 8 * i : 8 * i + 8, cols]
            snd2[4 * i + par] = jnp.where(sub, out_rows, pltpu.roll(grad_rows, CAP, 0))
            snd2[4 * i + 2 + par] = jnp.where(sub, pltpu.roll(out_rows, CAP, 0), grad_rows)

    def return_copy(i):
        return pltpu.make_async_remote_copy(
            src_ref=snd2.at[i],
            dst_ref=rcv2.at[e],
            send_sem=f_sem.at[0, i],
            recv_sem=f_sem.at[1, e],
            device_id=(dp_of(zl, jnp.int32(i // 2), c), 2 * x + i % 2),
            device_id_type=MESH,
        )

    for i in range(ne):
        mine = jnp.logical_and(x == i // 2, e == 2 * x + i % 2)

        @pl.when(mine)
        def _():
            rcv2[e] = snd2[i]

        @pl.when(jnp.logical_not(mine))
        def _():
            return_copy(i).start()

    for i in range(ne):

        @pl.when(jnp.logical_not(jnp.logical_and(to_self, e == i)))
        def _():
            arrived(rcv2.at[i], f_sem.at[1, i])

    home = rcv2[...].reshape(ne * 2 * CAP, feat).astype(BF16)
    mixed = gates_ref[:, 0:1] * dot(p0_out, home) + gates_ref[:, 1:2] * dot(p1_out, home)
    mixed_ref[...] = mixed.astype(BF16)
    gtok_ref[...] = dot(p0_grad + p1_grad, home).astype(BF16)

    for copy in sent:
        copy.wait_send()
    for i in range(ne):

        @pl.when(jnp.logical_not(jnp.logical_and(to_self, e == i)))
        def _():
            dispatch_copy(i).wait_send()

        @pl.when(jnp.logical_not(jnp.logical_and(x == i // 2, e == 2 * x + i % 2)))
        def _():
            return_copy(i).wait_send()

    for copy in loads:
        copy.wait()


def per_device(tokens, cotangent, route, gates, w_gate, w_up, w_down):
    nz = lax.axis_size("dp") // (NX * NC)
    ne = lax.axis_size("expert")
    feat = tokens.shape[1]
    chunk = 2 * feat
    hidden = w_gate.shape[1]
    rows = nz * NC * ROWS
    dma = pltpu.SemaphoreType.DMA
    vmem = pl.BlockSpec(memory_space=pltpu.VMEM)
    hbm = pl.BlockSpec(memory_space=pl.ANY)
    weight = jax.ShapeDtypeStruct(w_gate.shape, BF16)
    return pl.pallas_call(
        functools.partial(kernel, nz, ne),
        out_shape=(
            jax.ShapeDtypeStruct(tokens.shape, BF16),
            jax.ShapeDtypeStruct(tokens.shape, BF16),
            weight,
            weight,
            weight,
        ),
        in_specs=[vmem] * 4 + [hbm] * 3,
        out_specs=(vmem, vmem, hbm, hbm, hbm),
        scratch_shapes=[
            pltpu.VMEM((ne, 2 * CAP, feat), F32),
            pltpu.VMEM((ne, 2 * CAP, feat), F32),
            pltpu.VMEM((2, NX, NC, nz, ROWS, chunk), BF16),
            pltpu.VMEM((NX, hidden, chunk), BF16),
            pltpu.VMEM((NX, hidden, chunk), BF16),
            pltpu.VMEM((NX, hidden, chunk), BF16),
            pltpu.VMEM((3, rows, hidden), F32),
            pltpu.VMEM((3, rows, hidden), BF16),
            pltpu.VMEM((2, NX, NC, nz, ROWS, chunk), BF16),
            pltpu.VMEM((2, NX, nz, ROWS, chunk), BF16),
            pltpu.VMEM((2, nz, ROWS, chunk), BF16),
            pltpu.VMEM((2, 2, nz, ROWS, chunk), BF16),
            pltpu.VMEM((nz, 2, ROWS, chunk), BF16),
            pltpu.VMEM((nz, 2, ROWS, chunk), BF16),
            pltpu.VMEM((ne, 2 * CAP, feat), F32),
            pltpu.VMEM((ne, 2 * CAP, feat), F32),
            pltpu.VMEM((NX, hidden, chunk), BF16),
            pltpu.VMEM((NX, hidden, chunk), BF16),
            pltpu.VMEM((NX, hidden, chunk), BF16),
            dma((3 * NX,)),
            dma((3 * NX,)),
            dma((64,)),
            dma((2, ne)),
            dma((nz,)),
            dma((4, nz // 2)),
            dma((4, nz // 2)),
            dma((8,)),
            dma((nz,)),
            dma((2, ne)),
        ],
        compiler_params=pltpu.CompilerParams(
            collective_id=0, has_side_effects=True, vmem_limit_bytes=48 << 20
        ),
        name="expert_layer",
    )(tokens, cotangent, route, gates, w_gate, w_up, w_down)


def solution(mesh):
    return jax.shard_map(
        per_device,
        mesh=mesh,
        in_specs=(
            P("dp", "expert"),
            P("dp", "expert"),
            P("dp", None),
            P("dp", None),
            P("expert", "dp", None),
            P("expert", "dp", None),
            P("expert", "dp", None),
        ),
        out_specs=(
            P("dp", "expert"),
            P("dp", "expert"),
            P("expert", "dp", None),
            P("expert", "dp", None),
            P("expert", "dp", None),
        ),
        check_vma=False,
    )
```

```python
import functools

import jax
import jax.numpy as jnp
from jax import lax
from jax.experimental import pallas as pl
from jax.experimental.pallas import tpu as pltpu
from jax.sharding import PartitionSpec as P

MESH = pl.DeviceIdType.MESH
BF16 = jnp.bfloat16
F32 = jnp.float32
NX = 4
NC = 2
NY = 4
NS = 2
NZ = 8
RING = NS * NZ
CAP = 4
ROWS = NX * CAP
QUAD = 4


def dot(left, right):
    return jnp.dot(left, right, preferred_element_type=F32)


def dot_cols(left, right):
    return lax.dot_general(left, right, (((1,), (1,)), ((), ())), preferred_element_type=F32)


def dot_rows(left, right):
    return lax.dot_general(left, right, (((0,), (0,)), ((), ())), preferred_element_type=F32)


def layer_kernel(
    tok_ref,
    cot_ref,
    route_ref,
    gates_ref,
    wg_hbm,
    wu_hbm,
    wd_hbm,
    mixed_ref,
    gtok_ref,
    gg_hbm,
    gu_hbm,
    gd_hbm,
    snd,
    rcv,
    uz,
    g,
    wg,
    wu,
    wd,
    hid,
    part,
    sib,
    xr,
    zbuf,
    rz,
    snd2,
    rcv2,
    gg,
    gu,
    gd,
    w_sem,
    o_sem,
    send_sem,
    d_sem,
    z_sem,
    x_sem,
    c_sem,
    s_sem,
    r_sem,
    q_sem,
    f_sem,
):
    p = lax.axis_index("dp")
    e = lax.axis_index("expert")
    zl = lax.div(p, NX * NC)
    x = lax.rem(lax.div(p, NC), NX)
    c = lax.rem(p, NC)
    zh = lax.div(e, NY)
    y = lax.rem(e, NY)
    ring = zh * NZ + zl
    other = 1 - c
    rows = NC * NZ * ROWS
    toks, feat = tok_ref.shape
    peers = [lax.rem(x + k, NX) for k in (1, 3, 2)]

    def device(xx, yy, cc):
        return (zl * (NX * NC) + xx * NC + cc, zh * NY + yy)

    def along_z(to):
        low = lax.rem(to, NZ)
        return (low * (NX * NC) + x * NC + c, lax.div(to, NZ) * NY + y)

    dev_peers = [device(xx, y, c) for xx in peers]
    dev_sib = device(x, y, other)
    sent = []

    def send(src, dst, rsem, to):
        copy = pltpu.make_async_remote_copy(
            src_ref=src,
            dst_ref=dst,
            send_sem=send_sem.at[len(sent)],
            recv_sem=rsem,
            device_id=to,
            device_id_type=MESH,
        )
        copy.start()
        sent.append(copy)

    def arrived(dst, rsem):
        pltpu.make_async_remote_copy(
            src_ref=dst,
            dst_ref=dst,
            send_sem=send_sem.at[0],
            recv_sem=rsem,
            device_id=dev_sib,
            device_id_type=MESH,
        ).wait_recv()

    barrier = pltpu.get_barrier_semaphore()

    def greet(to):
        pl.semaphore_signal(barrier, inc=1, device_id=to, device_id_type=MESH)

    around = []
    for d in range(1, RING // 2 + 1):
        around.append(lax.rem(ring + d, RING))
        if d < RING // 2:
            around.append(lax.rem(ring + RING - d, RING))
    for to in reversed(around):
        greet(along_z(to))
    diagonal = x == y
    for i in range(NY):

        @pl.when(jnp.logical_not(jnp.logical_and(diagonal, y == i)))
        def _():
            greet(device(y, jnp.int32(i), c))

        @pl.when(jnp.logical_not(jnp.logical_and(diagonal, x == i)))
        def _():
            greet(device(jnp.int32(i), x, c))

    for to in dev_peers:
        greet(to)
    greet(dev_sib)

    loads = []
    for n, (hbm, vmem) in enumerate(((wg_hbm, wg), (wu_hbm, wu), (wd_hbm, wd))):
        copy = pltpu.make_async_copy(hbm.at[0], vmem, w_sem.at[n])
        copy.start()
        loads.append(copy)

    lane = lax.broadcasted_iota(jnp.int32, (toks, NY * NS * 2 * CAP), 1)
    lane_e = ((lane >> 3) & 1) * NY + (lane >> 4)
    first = ((lane >> 2) & 1) == 0
    lane_c = (lane & 3).astype(F32)
    m0 = (route_ref[:, 0:1] == lane_e).astype(F32)
    m1 = (route_ref[:, 1:2] == lane_e).astype(F32)
    earlier = (
        lax.broadcasted_iota(jnp.int32, (toks, toks), 1)
        < lax.broadcasted_iota(jnp.int32, (toks, toks), 0)
    ).astype(F32)
    before = dot(earlier, m0 + m1)
    p0 = jnp.where(before == lane_c, m0, 0.0)
    p1 = jnp.where(before + m0 == lane_c, m1, 0.0)
    p0_out = jnp.where(first, p0, 0.0).astype(BF16)
    p1_out = jnp.where(first, p1, 0.0).astype(BF16)
    p0_grad = jnp.where(first, 0.0, p0).astype(BF16)
    p1_grad = jnp.where(first, 0.0, p1).astype(BF16)
    cot = cot_ref[...].astype(F32)
    weighted0 = (gates_ref[:, 0:1] * cot).astype(BF16)
    weighted1 = (gates_ref[:, 1:2] * cot).astype(BF16)
    placed = (
        dot_rows(p0_out + p1_out, tok_ref[...])
        + dot_rows(p0_grad, weighted0)
        + dot_rows(p1_grad, weighted1)
    )
    snd[...] = placed.reshape(NY, NS * 2 * CAP, feat)

    near = jnp.where(diagonal, 2 * NY - 2, 2 * NY)
    pl.semaphore_wait(barrier, near + (RING - 1) + (NX - 1) + 1)

    def dispatch_copy(i):
        return pltpu.make_async_remote_copy(
            src_ref=snd.at[i],
            dst_ref=rcv.at[x],
            send_sem=d_sem.at[0, i],
            recv_sem=d_sem.at[1, x],
            device_id=device(y, jnp.int32(i), c),
            device_id_type=MESH,
        )

    for i in range(NY):
        mine = jnp.logical_and(diagonal, y == i)

        @pl.when(mine)
        def _():
            rcv[x] = snd[i]

        @pl.when(jnp.logical_not(mine))
        def _():
            dispatch_copy(i).start()

    for i in range(NX):

        @pl.when(jnp.logical_not(jnp.logical_and(diagonal, x == i)))
        def _():
            arrived(rcv.at[i], d_sem.at[1, i])

    sub = lax.broadcasted_iota(jnp.int32, (2 * CAP, feat), 0) < CAP
    for s in range(NS):
        t = [rcv[i, 2 * CAP * s : 2 * CAP * (s + 1)] for i in range(NX)]
        r = [pltpu.roll(v, CAP, 0) for v in t]
        xs_rows = [jnp.where(sub, t[0], r[1]), jnp.where(sub, t[2], r[3])]
        dy_rows = [jnp.where(sub, r[0], t[1]), jnp.where(sub, r[2], t[3])]
        uz[s, 0] = jnp.concatenate(xs_rows, axis=0).astype(BF16)
        uz[s, 1] = jnp.concatenate(dy_rows, axis=0).astype(BF16)

    for to in around:
        send(uz.at[lax.div(to, NZ)], g.at[:, x, zh, c, zl], z_sem.at[ring], along_z(to))
    g[:, x, zh, c, zl] = uz[zh]

    q = lax.div(ring, QUAD)
    quads = [lax.rem(q + k, RING // QUAD) for k in (0, 1, 3, 2)]

    def span(n):
        return lax.div(quads[n], NS), pl.ds(QUAD * lax.rem(quads[n], NS), QUAD)

    def region(xi, cc, n):
        s, zs = span(n)
        return g.at[:, xi, s, cc, zs]

    def stage_a(n):
        for j in range(QUAD):
            if n == 0:
                if j == 0:
                    continue
                src = QUAD * q + lax.rem(ring + j, QUAD)
            else:
                src = QUAD * quads[n] + j
            arrived(g.at[:, x, lax.div(src, NZ), c, lax.rem(src, NZ)], z_sem.at[src])
        for i in range(NX - 1):
            send(region(x, c, n), region(x, c, n), x_sem.at[i, n], dev_peers[i])
        send(region(x, c, n), region(x, c, n), c_sem.at[NX - 1, n], dev_sib)

    sources = [peers[1], peers[0], peers[2]]

    def stage_b(n):
        for i in range(NX - 1):
            arrived(region(sources[i], c, n), x_sem.at[i, n])
            send(region(sources[i], c, n), region(sources[i], c, n), c_sem.at[i, n], dev_sib)

    nq = RING // QUAD
    for n in range(nq + 1):
        if n < nq:
            stage_a(n)
        if n >= 1:
            stage_b(n - 1)

    for copy in loads:
        copy.wait()
    for n in range(nq):
        for i in range(NX - 1):
            arrived(region(sources[i], other, n), c_sem.at[i, n])
        arrived(region(x, other, n), c_sem.at[NX - 1, n])

    def cols(xi, s):
        start = (s * NX + xi) * feat
        return slice(start, start + feat)

    def rows_of(a, xi, s):
        return g[a, xi, s].reshape(rows, feat)

    slices = [(xi, s) for xi in range(NX) for s in range(NS)]
    pre_gate = sum(dot_cols(rows_of(0, *i), wg[:, cols(*i)]) for i in slices)
    pre_up = sum(dot_cols(rows_of(0, *i), wu[:, cols(*i)]) for i in slices)
    grad_hidden = sum(dot_cols(rows_of(1, *i), wd[:, cols(*i)]) for i in slices)
    sig = jax.nn.sigmoid(pre_gate)
    silu = pre_gate * sig
    hid[0] = (silu * pre_up).astype(BF16)
    hid[1] = (grad_hidden * pre_up * sig * (1.0 + pre_gate * (1.0 - sig))).astype(BF16)
    hid[2] = (grad_hidden * silu).astype(BF16)

    for xi, s in slices:
        y0 = dot(hid[0], wd[:, cols(xi, s)])
        y1 = dot(hid[1], wg[:, cols(xi, s)]) + dot(hid[2], wu[:, cols(xi, s)])
        part[0, xi, s] = y0.astype(BF16).reshape(NC, NZ, ROWS, feat)
        part[1, xi, s] = y1.astype(BF16).reshape(NC, NZ, ROWS, feat)
    for n in reversed(range(nq)):
        s, zs = span(n)
        send(part.at[:, :, s, other, zs], sib.at[:, :, s, zs], s_sem.at[n], dev_sib)

    def chip_sum(xi, s, zs):
        return part[:, xi, s, c, zs].astype(F32) + sib[:, xi, s, zs].astype(F32)

    for n in reversed(range(nq)):
        s, zs = span(n)
        arrived(sib.at[:, :, s, zs], s_sem.at[n])
        for i in (2, 0, 1):
            xi = peers[i]
            part[:, xi, s, c, zs] = chip_sum(xi, s, zs).astype(BF16)
            send(part.at[:, xi, s, c, zs], xr.at[i, :, s, zs], r_sem.at[i, n], dev_peers[i])

    for xi, s in slices:
        gd[:, cols(xi, s)] = dot_rows(hid[0], rows_of(1, xi, s)).astype(BF16)
        gg[:, cols(xi, s)] = dot_rows(hid[1], rows_of(0, xi, s)).astype(BF16)
        gu[:, cols(xi, s)] = dot_rows(hid[2], rows_of(0, xi, s)).astype(BF16)
    stores = []
    for n, (vmem, hbm) in enumerate(((gd, gd_hbm), (gg, gg_hbm), (gu, gu_hbm))):
        copy = pltpu.make_async_copy(vmem, hbm.at[0], o_sem.at[n])
        copy.start()
        stores.append(copy)

    for n in reversed(range(nq)):
        s, zs = span(n)
        total = chip_sum(x, s, zs)
        for i in range(NX - 1):
            arrived(xr.at[i, :, s, zs], r_sem.at[i, n])
            total = total + xr[i, :, s, zs].astype(F32)
        for a in range(2):
            zbuf[pl.ds(QUAD * quads[n], QUAD), a] = total[a].astype(BF16)
        for j in range(QUAD):
            if n == 0:
                if j == 0:
                    continue
                to = QUAD * q + lax.rem(ring + j, QUAD)
            else:
                to = QUAD * quads[n] + j
            send(zbuf.at[to], rz.at[ring], q_sem.at[ring], along_z(to))
    rz[ring] = zbuf[ring]
    for src in around:
        arrived(rz.at[src], q_sem.at[src])

    for s in range(NS):
        total = rz[s * NZ].astype(F32)
        for z in range(1, NZ):
            total = total + rz[s * NZ + z].astype(F32)
        total = total.astype(BF16).astype(F32)
        block = slice(2 * CAP * s, 2 * CAP * (s + 1))
        for i in range(2):
            out_rows = total[0, 8 * i : 8 * i + 8]
            grad_rows = total[1, 8 * i : 8 * i + 8]
            snd2[2 * i, block] = jnp.where(sub, out_rows, pltpu.roll(grad_rows, CAP, 0))
            snd2[2 * i + 1, block] = jnp.where(sub, pltpu.roll(out_rows, CAP, 0), grad_rows)

    def return_copy(i):
        return pltpu.make_async_remote_copy(
            src_ref=snd2.at[i],
            dst_ref=rcv2.at[y],
            send_sem=f_sem.at[0, i],
            recv_sem=f_sem.at[1, y],
            device_id=device(jnp.int32(i), x, c),
            device_id_type=MESH,
        )

    for i in range(NX):
        mine = jnp.logical_and(diagonal, x == i)

        @pl.when(mine)
        def _():
            rcv2[y] = snd2[i]

        @pl.when(jnp.logical_not(mine))
        def _():
            return_copy(i).start()

    for i in range(NY):

        @pl.when(jnp.logical_not(jnp.logical_and(diagonal, y == i)))
        def _():
            arrived(rcv2.at[i], f_sem.at[1, i])

    home = rcv2[...].reshape(NY * NS * 2 * CAP, feat).astype(BF16)
    mixed = gates_ref[:, 0:1] * dot(p0_out, home) + gates_ref[:, 1:2] * dot(p1_out, home)
    mixed_ref[...] = mixed.astype(BF16)
    gtok_ref[...] = dot(p0_grad + p1_grad, home).astype(BF16)

    for copy in stores:
        copy.wait()
    for copy in sent:
        copy.wait_send()
    for i in range(NY):

        @pl.when(jnp.logical_not(jnp.logical_and(diagonal, y == i)))
        def _():
            dispatch_copy(i).wait_send()

        @pl.when(jnp.logical_not(jnp.logical_and(diagonal, x == i)))
        def _():
            return_copy(i).wait_send()


def store_kernel(n, *refs):
    copies = [
        pltpu.make_async_copy(refs[i], refs[n + i], refs[2 * n].at[i]) for i in range(n)
    ]
    for copy in copies:
        copy.start()
    for copy in copies:
        copy.wait()


def per_device(tokens, cotangent, route, gates, w_gate, w_up, w_down):
    assert lax.axis_size("dp") == NZ * NX * NC and lax.axis_size("expert") == NS * NY
    feat = tokens.shape[1]
    hidden = w_gate.shape[1]
    rows = NC * NZ * ROWS
    dma = pltpu.SemaphoreType.DMA
    vmem = pl.BlockSpec(memory_space=pltpu.VMEM)
    hbm = pl.BlockSpec(memory_space=pl.ANY)
    outs = (jax.ShapeDtypeStruct(tokens.shape, BF16),) * 2
    outs += (jax.ShapeDtypeStruct(w_gate.shape, BF16),) * 3
    nq = RING // QUAD
    results = pl.pallas_call(
        layer_kernel,
        out_shape=outs,
        in_specs=[vmem] * 4 + [hbm] * 3,
        out_specs=(vmem, vmem, hbm, hbm, hbm),
        scratch_shapes=[
            pltpu.VMEM((NY, NS * 2 * CAP, feat), F32),
            pltpu.VMEM((NX, NS * 2 * CAP, feat), F32),
            pltpu.VMEM((NS, 2, ROWS, feat), BF16),
            pltpu.VMEM((2, NX, NS, NC, NZ, ROWS, feat), BF16),
            pltpu.VMEM(w_gate.shape[1:], BF16),
            pltpu.VMEM(w_gate.shape[1:], BF16),
            pltpu.VMEM(w_gate.shape[1:], BF16),
            pltpu.VMEM((3, rows, hidden), BF16),
            pltpu.VMEM((2, NX, NS, NC, NZ, ROWS, feat), BF16),
            pltpu.VMEM((2, NX, NS, NZ, ROWS, feat), BF16),
            pltpu.VMEM((NX - 1, 2, NS, NZ, ROWS, feat), BF16),
            pltpu.VMEM((RING, 2, ROWS, feat), BF16),
            pltpu.VMEM((RING, 2, ROWS, feat), BF16),
            pltpu.VMEM((NX, NS * 2 * CAP, feat), F32),
            pltpu.VMEM((NY, NS * 2 * CAP, feat), F32),
            pltpu.VMEM(w_gate.shape[1:], BF16),
            pltpu.VMEM(w_gate.shape[1:], BF16),
            pltpu.VMEM(w_gate.shape[1:], BF16),
            dma((3,)),
            dma((3,)),
            dma((96,)),
            dma((2, NY)),
            dma((RING,)),
            dma((NX - 1, nq)),
            dma((NX, nq)),
            dma((nq,)),
            dma((NX - 1, nq)),
            dma((RING,)),
            dma((2, NY)),
        ],
        compiler_params=pltpu.CompilerParams(
            collective_id=0, has_side_effects=True, vmem_limit_bytes=62 << 20
        ),
        name="expert_layer",
    )(tokens, cotangent, route, gates, w_gate, w_up, w_down)
    return pl.pallas_call(
        functools.partial(store_kernel, len(outs)),
        out_shape=outs,
        in_specs=[hbm] * len(outs),
        out_specs=(hbm,) * len(outs),
        scratch_shapes=[dma((len(outs),))],
        compiler_params=pltpu.CompilerParams(vmem_limit_bytes=62 << 20),
        name="store_results",
    )(*results)


def solution(mesh):
    return jax.shard_map(
        per_device,
        mesh=mesh,
        in_specs=(
            P("dp", "expert"),
            P("dp", "expert"),
            P("dp", None),
            P("dp", None),
            P("expert", "dp", None),
            P("expert", "dp", None),
            P("expert", "dp", None),
        ),
        out_specs=(
            P("dp", "expert"),
            P("dp", "expert"),
            P("expert", "dp", None),
            P("expert", "dp", None),
            P("expert", "dp", None),
        ),
        check_vma=False,
    )
```

```python
import functools

import jax
import jax.numpy as jnp
from jax import lax
from jax.experimental import pallas as pl
from jax.experimental.pallas import tpu as pltpu
from jax.sharding import PartitionSpec as P

MESH = pl.DeviceIdType.MESH
BF16 = jnp.bfloat16
F32 = jnp.float32
NX = 4
NC = 2
NY = 4
NS = 2
NZ = 8
RING = NS * NZ
CAP = 4
ROWS = NX * CAP
QUAD = 4


def dot(left, right):
    return jnp.dot(left, right, preferred_element_type=F32)


def dot_cols(left, right):
    return lax.dot_general(left, right, (((1,), (1,)), ((), ())), preferred_element_type=F32)


def dot_rows(left, right):
    return lax.dot_general(left, right, (((0,), (0,)), ((), ())), preferred_element_type=F32)


def layer_kernel(
    tok_ref,
    cot_ref,
    route_ref,
    gates_ref,
    wg_hbm,
    wu_hbm,
    wd_hbm,
    mixed_ref,
    gtok_ref,
    gg_hbm,
    gu_hbm,
    gd_hbm,
    snd,
    rcv,
    uz,
    g,
    wg,
    wu,
    wd,
    hid,
    part,
    sib,
    xr,
    zbuf,
    rz,
    snd2,
    rcv2,
    gg,
    gu,
    gd,
    w_sem,
    o_sem,
    send_sem,
    d_sem,
    z_sem,
    x_sem,
    c_sem,
    s_sem,
    r_sem,
    q_sem,
    f_sem,
):
    p = lax.axis_index("dp")
    e = lax.axis_index("expert")
    zl = lax.div(p, NX * NC)
    x = lax.rem(lax.div(p, NC), NX)
    c = lax.rem(p, NC)
    zh = lax.div(e, NY)
    y = lax.rem(e, NY)
    ring = zh * NZ + zl
    other = 1 - c
    rows = NC * NZ * ROWS
    toks, feat = tok_ref.shape
    peers = [lax.rem(x + k, NX) for k in (1, 3, 2)]

    def device(xx, yy, cc):
        return (zl * (NX * NC) + xx * NC + cc, zh * NY + yy)

    def along_z(to):
        low = lax.rem(to, NZ)
        return (low * (NX * NC) + x * NC + c, lax.div(to, NZ) * NY + y)

    dev_peers = [device(xx, y, c) for xx in peers]
    dev_sib = device(x, y, other)
    sent = []

    def send(src, dst, rsem, to):
        copy = pltpu.make_async_remote_copy(
            src_ref=src,
            dst_ref=dst,
            send_sem=send_sem.at[len(sent)],
            recv_sem=rsem,
            device_id=to,
            device_id_type=MESH,
        )
        copy.start()
        sent.append(copy)

    def arrived(dst, rsem):
        pltpu.make_async_remote_copy(
            src_ref=dst,
            dst_ref=dst,
            send_sem=send_sem.at[0],
            recv_sem=rsem,
            device_id=dev_sib,
            device_id_type=MESH,
        ).wait_recv()

    barrier = pltpu.get_barrier_semaphore()

    def greet(to):
        pl.semaphore_signal(barrier, inc=1, device_id=to, device_id_type=MESH)

    around = []
    for d in range(1, RING // 2 + 1):
        around.append(lax.rem(ring + d, RING))
        if d < RING // 2:
            around.append(lax.rem(ring + RING - d, RING))
    for to in reversed(around):
        greet(along_z(to))
    diagonal = x == y
    for i in range(NY):

        @pl.when(jnp.logical_not(jnp.logical_and(diagonal, y == i)))
        def _():
            greet(device(y, jnp.int32(i), c))

        @pl.when(jnp.logical_not(jnp.logical_and(diagonal, x == i)))
        def _():
            greet(device(jnp.int32(i), x, c))

    for to in dev_peers:
        greet(to)
    greet(dev_sib)

    loads = []
    for n, (hbm, vmem) in enumerate(((wg_hbm, wg), (wu_hbm, wu), (wd_hbm, wd))):
        copy = pltpu.make_async_copy(hbm.at[0], vmem, w_sem.at[n])
        copy.start()
        loads.append(copy)

    picks = NY * NS * 2 * CAP
    row = lax.broadcasted_iota(jnp.int32, (picks, toks), 0)
    row_e = ((row >> 3) & 1) * NY + (row >> 4)
    row_c = (row & 3).astype(F32)
    m0 = (route_ref[0:1, :] == row_e).astype(F32)
    m1 = (route_ref[1:2, :] == row_e).astype(F32)
    earlier = (
        lax.broadcasted_iota(jnp.int32, (toks, toks), 0)
        < lax.broadcasted_iota(jnp.int32, (toks, toks), 1)
    ).astype(F32)
    before = dot(m0 + m1, earlier)
    p0 = jnp.where(before == row_c, m0, 0.0)
    p1 = jnp.where(before + m0 == row_c, m1, 0.0)
    both = p0 + p1
    gate = jnp.sum(p0 * gates_ref[0:1, :] + p1 * gates_ref[1:2, :], axis=1, keepdims=True)
    first = ((lax.broadcasted_iota(jnp.int32, (picks, feat), 0) >> 2) & 1) == 0
    pick = both.astype(BF16)
    placed_grad = (gate * dot(pick, cot_ref[...])).astype(BF16).astype(F32)
    placed = jnp.where(first, dot(pick, tok_ref[...]), placed_grad)
    snd[...] = placed.reshape(NY, NS * 2 * CAP, feat)

    near = jnp.where(diagonal, 2 * NY - 2, 2 * NY)
    pl.semaphore_wait(barrier, near + (RING - 1) + (NX - 1) + 1)

    def dispatch_copy(i):
        return pltpu.make_async_remote_copy(
            src_ref=snd.at[i],
            dst_ref=rcv.at[x],
            send_sem=d_sem.at[0, i],
            recv_sem=d_sem.at[1, x],
            device_id=device(y, jnp.int32(i), c),
            device_id_type=MESH,
        )

    for i in range(NY):
        mine = jnp.logical_and(diagonal, y == i)

        @pl.when(mine)
        def _():
            rcv[x] = snd[i]

        @pl.when(jnp.logical_not(mine))
        def _():
            dispatch_copy(i).start()

    for i in range(NX):

        @pl.when(jnp.logical_not(jnp.logical_and(diagonal, x == i)))
        def _():
            arrived(rcv.at[i], d_sem.at[1, i])

    sub = lax.broadcasted_iota(jnp.int32, (2 * CAP, feat), 0) < CAP
    for s in range(NS):
        t = [rcv[i, 2 * CAP * s : 2 * CAP * (s + 1)] for i in range(NX)]
        r = [pltpu.roll(v, CAP, 0) for v in t]
        xs_rows = [jnp.where(sub, t[0], r[1]), jnp.where(sub, t[2], r[3])]
        dy_rows = [jnp.where(sub, r[0], t[1]), jnp.where(sub, r[2], t[3])]
        uz[s, 0] = jnp.concatenate(xs_rows, axis=0).astype(BF16)
        uz[s, 1] = jnp.concatenate(dy_rows, axis=0).astype(BF16)

    def send_unit(to):
        send(uz.at[lax.div(to, NZ)], g.at[:, x, zh, c, zl], z_sem.at[ring], along_z(to))

    q = lax.div(ring, QUAD)
    mates = [QUAD * q + lax.rem(ring + j, QUAD) for j in range(1, QUAD)]
    across = lax.rem(ring + RING // 2, RING)
    send_unit(across)
    for to in mates:
        send_unit(to)
    for k in (1, 3):
        for j in range(QUAD):
            send_unit(QUAD * lax.rem(q + k, RING // QUAD) + lax.rem(ring + j, QUAD))
    g[:, x, zh, c, zl] = uz[zh]

    def unit(src):
        return g.at[:, x, lax.div(src, NZ), c, lax.rem(src, NZ)]

    quads = [lax.rem(q + k, RING // QUAD) for k in (0, 1, 3, 2)]

    def span(n):
        return lax.div(quads[n], NS), pl.ds(QUAD * lax.rem(quads[n], NS), QUAD)

    def region(xi, cc, n):
        s, zs = span(n)
        return g.at[:, xi, s, cc, zs]

    def pass_on():
        arrived(unit(across), z_sem.at[across])
        for to in mates:
            send(unit(across), unit(across), z_sem.at[across], along_z(to))

    def stage_a(n):
        for j in range(QUAD):
            src = QUAD * quads[n] + lax.rem(ring + j, QUAD)
            if j > 0 or n in (1, 2):
                arrived(unit(src), z_sem.at[src])
        for i in range(NX - 1):
            send(region(x, c, n), region(x, c, n), x_sem.at[i, n], dev_peers[i])
        send(region(x, c, n), region(x, c, n), c_sem.at[NX - 1, n], dev_sib)

    sources = [peers[1], peers[0], peers[2]]

    def stage_b(n):
        for i in range(NX - 1):
            arrived(region(sources[i], c, n), x_sem.at[i, n])
            send(region(sources[i], c, n), region(sources[i], c, n), c_sem.at[i, n], dev_sib)

    nq = RING // QUAD
    stage_a(0)
    stage_a(1)
    pass_on()
    stage_b(0)
    stage_a(2)
    stage_b(1)
    stage_a(3)
    stage_b(2)
    stage_b(3)

    for copy in loads:
        copy.wait()
    for n in range(nq):
        for i in range(NX - 1):
            arrived(region(sources[i], other, n), c_sem.at[i, n])
        arrived(region(x, other, n), c_sem.at[NX - 1, n])

    def cols(xi, s):
        start = (s * NX + xi) * feat
        return slice(start, start + feat)

    def rows_of(a, xi, s):
        return g[a, xi, s].reshape(rows, feat)

    slices = [(xi, s) for xi in range(NX) for s in range(NS)]
    pre_gate = sum(dot_cols(rows_of(0, *i), wg[:, cols(*i)]) for i in slices)
    pre_up = sum(dot_cols(rows_of(0, *i), wu[:, cols(*i)]) for i in slices)
    grad_hidden = sum(dot_cols(rows_of(1, *i), wd[:, cols(*i)]) for i in slices)
    sig = jax.nn.sigmoid(pre_gate)
    silu = pre_gate * sig
    hid[0] = (silu * pre_up).astype(BF16)
    hid[1] = (grad_hidden * pre_up * sig * (1.0 + pre_gate * (1.0 - sig))).astype(BF16)
    hid[2] = (grad_hidden * silu).astype(BF16)

    for xi, s in slices:
        y0 = dot(hid[0], wd[:, cols(xi, s)])
        y1 = dot(hid[1], wg[:, cols(xi, s)]) + dot(hid[2], wu[:, cols(xi, s)])
        part[0, xi, s] = y0.astype(BF16).reshape(NC, NZ, ROWS, feat)
        part[1, xi, s] = y1.astype(BF16).reshape(NC, NZ, ROWS, feat)
    for n in reversed(range(nq)):
        s, zs = span(n)
        send(part.at[:, :, s, other, zs], sib.at[:, :, s, zs], s_sem.at[n], dev_sib)

    def chip_sum(xi, s, zs):
        return part[:, xi, s, c, zs].astype(F32) + sib[:, xi, s, zs].astype(F32)

    for n in reversed(range(nq)):
        s, zs = span(n)
        arrived(sib.at[:, :, s, zs], s_sem.at[n])
        for i in (2, 0, 1):
            xi = peers[i]
            part[:, xi, s, c, zs] = chip_sum(xi, s, zs).astype(BF16)
            send(part.at[:, xi, s, c, zs], xr.at[i, :, s, zs], r_sem.at[i, n], dev_peers[i])

    for xi, s in slices:
        gd[:, cols(xi, s)] = dot_rows(hid[0], rows_of(1, xi, s)).astype(BF16)
        gg[:, cols(xi, s)] = dot_rows(hid[1], rows_of(0, xi, s)).astype(BF16)
        gu[:, cols(xi, s)] = dot_rows(hid[2], rows_of(0, xi, s)).astype(BF16)
    stores = []
    for n, (vmem, hbm) in enumerate(((gd, gd_hbm), (gg, gg_hbm), (gu, gu_hbm))):
        copy = pltpu.make_async_copy(vmem, hbm.at[0], o_sem.at[n])
        copy.start()
        stores.append(copy)

    for n in reversed(range(nq)):
        s, zs = span(n)
        total = chip_sum(x, s, zs)
        for i in range(NX - 1):
            arrived(xr.at[i, :, s, zs], r_sem.at[i, n])
            total = total + xr[i, :, s, zs].astype(F32)
        for a in range(2):
            zbuf[pl.ds(QUAD * quads[n], QUAD), a] = total[a].astype(BF16)
        for j in range(QUAD):
            if n == 0:
                if j == 0:
                    continue
                to = QUAD * q + lax.rem(ring + j, QUAD)
            else:
                to = QUAD * quads[n] + j
            send(zbuf.at[to], rz.at[ring], q_sem.at[ring], along_z(to))
    rz[ring] = zbuf[ring]
    for src in around:
        arrived(rz.at[src], q_sem.at[src])

    for s in range(NS):
        total = rz[s * NZ].astype(F32)
        for z in range(1, NZ):
            total = total + rz[s * NZ + z].astype(F32)
        total = total.astype(BF16).astype(F32)
        block = slice(2 * CAP * s, 2 * CAP * (s + 1))
        for i in range(2):
            out_rows = total[0, 8 * i : 8 * i + 8]
            grad_rows = total[1, 8 * i : 8 * i + 8]
            snd2[2 * i, block] = jnp.where(sub, out_rows, pltpu.roll(grad_rows, CAP, 0))
            snd2[2 * i + 1, block] = jnp.where(sub, pltpu.roll(out_rows, CAP, 0), grad_rows)

    def return_copy(i):
        return pltpu.make_async_remote_copy(
            src_ref=snd2.at[i],
            dst_ref=rcv2.at[y],
            send_sem=f_sem.at[0, i],
            recv_sem=f_sem.at[1, y],
            device_id=device(jnp.int32(i), x, c),
            device_id_type=MESH,
        )

    for i in range(NX):
        mine = jnp.logical_and(diagonal, x == i)

        @pl.when(mine)
        def _():
            rcv2[y] = snd2[i]

        @pl.when(jnp.logical_not(mine))
        def _():
            return_copy(i).start()

    for i in range(NY):

        @pl.when(jnp.logical_not(jnp.logical_and(diagonal, y == i)))
        def _():
            arrived(rcv2.at[i], f_sem.at[1, i])

    home = rcv2[...].reshape(picks, feat)
    out_pick = jnp.where(first[:, :toks], both, 0.0)
    mixed_ref[...] = lax.dot_general(
        out_pick,
        gate * home,
        (((0,), (0,)), ((), ())),
        precision=lax.Precision.HIGHEST,
        preferred_element_type=F32,
    ).astype(BF16)
    grad_pick = (both - out_pick).astype(BF16)
    gtok_ref[...] = dot_rows(grad_pick, home.astype(BF16)).astype(BF16)

    for copy in stores:
        copy.wait()
    for copy in sent:
        copy.wait_send()
    for i in range(NY):

        @pl.when(jnp.logical_not(jnp.logical_and(diagonal, y == i)))
        def _():
            dispatch_copy(i).wait_send()

        @pl.when(jnp.logical_not(jnp.logical_and(diagonal, x == i)))
        def _():
            return_copy(i).wait_send()


def store_kernel(n, *refs):
    ins, outs, bufs, (sems,) = refs[:n], refs[n : 2 * n], refs[2 * n : 3 * n], refs[3 * n :]
    loads = [pltpu.make_async_copy(ins[i], bufs[i], sems.at[0, i]) for i in range(n)]
    stores = [pltpu.make_async_copy(bufs[i], outs[i], sems.at[1, i]) for i in range(n)]
    for copy in loads:
        copy.start()
    for load, store in zip(loads, stores):
        load.wait()
        store.start()
    for copy in stores:
        copy.wait()


def per_device(tokens, cotangent, route, gates, w_gate, w_up, w_down):
    assert lax.axis_size("dp") == NZ * NX * NC and lax.axis_size("expert") == NS * NY
    feat = tokens.shape[1]
    hidden = w_gate.shape[1]
    rows = NC * NZ * ROWS
    dma = pltpu.SemaphoreType.DMA
    vmem = pl.BlockSpec(memory_space=pltpu.VMEM)
    hbm = pl.BlockSpec(memory_space=pl.ANY)
    outs = (jax.ShapeDtypeStruct(tokens.shape, BF16),) * 2
    outs += (jax.ShapeDtypeStruct(w_gate.shape, BF16),) * 3
    nq = RING // QUAD
    results = pl.pallas_call(
        layer_kernel,
        out_shape=outs,
        in_specs=[vmem] * 4 + [hbm] * 3,
        out_specs=(vmem, vmem, hbm, hbm, hbm),
        scratch_shapes=[
            pltpu.VMEM((NY, NS * 2 * CAP, feat), F32),
            pltpu.VMEM((NX, NS * 2 * CAP, feat), F32),
            pltpu.VMEM((NS, 2, ROWS, feat), BF16),
            pltpu.VMEM((2, NX, NS, NC, NZ, ROWS, feat), BF16),
            pltpu.VMEM(w_gate.shape[1:], BF16),
            pltpu.VMEM(w_gate.shape[1:], BF16),
            pltpu.VMEM(w_gate.shape[1:], BF16),
            pltpu.VMEM((3, rows, hidden), BF16),
            pltpu.VMEM((2, NX, NS, NC, NZ, ROWS, feat), BF16),
            pltpu.VMEM((2, NX, NS, NZ, ROWS, feat), BF16),
            pltpu.VMEM((NX - 1, 2, NS, NZ, ROWS, feat), BF16),
            pltpu.VMEM((RING, 2, ROWS, feat), BF16),
            pltpu.VMEM((RING, 2, ROWS, feat), BF16),
            pltpu.VMEM((NX, NS * 2 * CAP, feat), F32),
            pltpu.VMEM((NY, NS * 2 * CAP, feat), F32),
            pltpu.VMEM(w_gate.shape[1:], BF16),
            pltpu.VMEM(w_gate.shape[1:], BF16),
            pltpu.VMEM(w_gate.shape[1:], BF16),
            dma((3,)),
            dma((3,)),
            dma((96,)),
            dma((2, NY)),
            dma((RING,)),
            dma((NX - 1, nq)),
            dma((NX, nq)),
            dma((nq,)),
            dma((NX - 1, nq)),
            dma((RING,)),
            dma((2, NY)),
        ],
        compiler_params=pltpu.CompilerParams(
            collective_id=0, has_side_effects=True, vmem_limit_bytes=62 << 20
        ),
        name="expert_layer",
    )(tokens, cotangent, route.T, gates.T, w_gate, w_up, w_down)
    return pl.pallas_call(
        functools.partial(store_kernel, len(outs)),
        out_shape=outs,
        in_specs=[hbm] * len(outs),
        out_specs=(hbm,) * len(outs),
        scratch_shapes=[pltpu.VMEM(out.shape, out.dtype) for out in outs] + [dma((2, len(outs)))],
        compiler_params=pltpu.CompilerParams(vmem_limit_bytes=62 << 20),
        name="store_results",
    )(*results)


def solution(mesh):
    return jax.shard_map(
        per_device,
        mesh=mesh,
        in_specs=(
            P("dp", "expert"),
            P("dp", "expert"),
            P("dp", None),
            P("dp", None),
            P("expert", "dp", None),
            P("expert", "dp", None),
            P("expert", "dp", None),
        ),
        out_specs=(
            P("dp", "expert"),
            P("dp", "expert"),
            P("expert", "dp", None),
            P("expert", "dp", None),
            P("expert", "dp", None),
        ),
        check_vma=False,
    )
```

```python
import functools

import jax
import jax.numpy as jnp
from jax import lax
from jax.experimental import pallas as pl
from jax.experimental.pallas import tpu as pltpu
from jax.sharding import PartitionSpec as P

MESH = pl.DeviceIdType.MESH
BF16 = jnp.bfloat16
F32 = jnp.float32
NX = 4
NC = 2
NY = 4
NS = 2
NZ = 8
RING = NS * NZ
CAP = 4
ROWS = NX * CAP
QUAD = 4


def dot(left, right):
    return jnp.dot(left, right, preferred_element_type=F32)


def dot_cols(left, right):
    return lax.dot_general(left, right, (((1,), (1,)), ((), ())), preferred_element_type=F32)


def dot_rows(left, right):
    return lax.dot_general(left, right, (((0,), (0,)), ((), ())), preferred_element_type=F32)


def layer_kernel(
    tok_ref,
    cot_ref,
    route_ref,
    gates_ref,
    wg_hbm,
    wu_hbm,
    wd_hbm,
    mixed_ref,
    gtok_ref,
    gg_hbm,
    gu_hbm,
    gd_hbm,
    snd,
    rcv,
    uz,
    g,
    wg,
    wu,
    wd,
    hid,
    part,
    sib,
    xr,
    zbuf,
    rz,
    snd2,
    rcv2,
    gg,
    gu,
    gd,
    w_sem,
    o_sem,
    send_sem,
    d_sem,
    z_sem,
    x_sem,
    c_sem,
    s_sem,
    r_sem,
    q_sem,
    f_sem,
    vouch,
):
    p = lax.axis_index("dp")
    e = lax.axis_index("expert")
    zl = lax.div(p, NX * NC)
    x = lax.rem(lax.div(p, NC), NX)
    c = lax.rem(p, NC)
    zh = lax.div(e, NY)
    y = lax.rem(e, NY)
    ring = zh * NZ + zl
    other = 1 - c
    rows = NC * NZ * ROWS
    toks, feat = tok_ref.shape
    peers = [lax.rem(x + k, NX) for k in (1, 3, 2)]

    def device(xx, yy, cc):
        return (zl * (NX * NC) + xx * NC + cc, zh * NY + yy)

    def along_z(to):
        low = lax.rem(to, NZ)
        return (low * (NX * NC) + x * NC + c, lax.div(to, NZ) * NY + y)

    dev_peers = [device(xx, y, c) for xx in peers]
    dev_sib = device(x, y, other)
    sent = []

    def send(src, dst, rsem, to):
        copy = pltpu.make_async_remote_copy(
            src_ref=src,
            dst_ref=dst,
            send_sem=send_sem.at[len(sent)],
            recv_sem=rsem,
            device_id=to,
            device_id_type=MESH,
        )
        copy.start()
        sent.append(copy)

    def arrived(dst, rsem):
        pltpu.make_async_remote_copy(
            src_ref=dst,
            dst_ref=dst,
            send_sem=send_sem.at[0],
            recv_sem=rsem,
            device_id=dev_sib,
            device_id_type=MESH,
        ).wait_recv()

    barrier = pltpu.get_barrier_semaphore()

    def greet(to):
        pl.semaphore_signal(barrier, inc=1, device_id=to, device_id_type=MESH)

    around = [lax.rem(ring + k, RING) for k in range(1, RING)]
    q = lax.div(ring, QUAD)
    mates = [QUAD * q + lax.rem(ring + j, QUAD) for j in range(1, QUAD)]
    across = [lax.rem(ring + k * QUAD, RING) for k in (2, 1, 3)]
    for to in across[1:] + mates:
        greet(along_z(to))
    diagonal = x == y
    for i in range(NY):

        @pl.when(jnp.logical_not(jnp.logical_and(diagonal, y == i)))
        def _():
            greet(device(y, jnp.int32(i), c))

        @pl.when(jnp.logical_not(jnp.logical_and(diagonal, x == i)))
        def _():
            greet(device(jnp.int32(i), x, c))

    for to in dev_peers:
        greet(to)
    greet(dev_sib)

    loads = []
    for n, (hbm, vmem) in enumerate(((wg_hbm, wg), (wu_hbm, wu), (wd_hbm, wd))):
        copy = pltpu.make_async_copy(hbm.at[0], vmem, w_sem.at[n])
        copy.start()
        loads.append(copy)

    picks = NY * NS * 2 * CAP
    row = lax.broadcasted_iota(jnp.int32, (picks, toks), 0)
    row_e = ((row >> 3) & 1) * NY + (row >> 4)
    row_c = (row & 3).astype(F32)
    m0 = (route_ref[0:1, :] == row_e).astype(F32)
    m1 = (route_ref[1:2, :] == row_e).astype(F32)
    earlier = (
        lax.broadcasted_iota(jnp.int32, (toks, toks), 0)
        < lax.broadcasted_iota(jnp.int32, (toks, toks), 1)
    ).astype(F32)
    before = dot(m0 + m1, earlier)
    p0 = jnp.where(before == row_c, m0, 0.0)
    p1 = jnp.where(before + m0 == row_c, m1, 0.0)
    both = p0 + p1
    gate = jnp.sum(p0 * gates_ref[0:1, :] + p1 * gates_ref[1:2, :], axis=1, keepdims=True)
    first = ((lax.broadcasted_iota(jnp.int32, (picks, feat), 0) >> 2) & 1) == 0
    pick = both.astype(BF16)
    placed_grad = (gate * dot(pick, cot_ref[...])).astype(BF16).astype(F32)
    placed = jnp.where(first, dot(pick, tok_ref[...]), placed_grad)
    snd[...] = placed.reshape(NY, NS * 2 * CAP, feat)

    near = jnp.where(diagonal, 2 * NY - 2, 2 * NY)
    pl.semaphore_wait(barrier, near + 2 + (QUAD - 1) + (NX - 1) + 1)

    pl.semaphore_signal(vouch, inc=1, device_id=along_z(across[2]), device_id_type=MESH)

    def dispatch_copy(i):
        return pltpu.make_async_remote_copy(
            src_ref=snd.at[i],
            dst_ref=rcv.at[x],
            send_sem=d_sem.at[0, i],
            recv_sem=d_sem.at[1, x],
            device_id=device(y, jnp.int32(i), c),
            device_id_type=MESH,
        )

    for i in range(NY):
        mine = jnp.logical_and(diagonal, y == i)

        @pl.when(mine)
        def _():
            rcv[x] = snd[i]

        @pl.when(jnp.logical_not(mine))
        def _():
            dispatch_copy(i).start()

    for i in range(NX):

        @pl.when(jnp.logical_not(jnp.logical_and(diagonal, x == i)))
        def _():
            arrived(rcv.at[i], d_sem.at[1, i])

    sub = lax.broadcasted_iota(jnp.int32, (2 * CAP, feat), 0) < CAP
    for s in range(NS):
        t = [rcv[i, 2 * CAP * s : 2 * CAP * (s + 1)] for i in range(NX)]
        r = [pltpu.roll(v, CAP, 0) for v in t]
        xs_rows = [jnp.where(sub, t[0], r[1]), jnp.where(sub, t[2], r[3])]
        dy_rows = [jnp.where(sub, r[0], t[1]), jnp.where(sub, r[2], t[3])]
        uz[s, 0] = jnp.concatenate(xs_rows, axis=0).astype(BF16)
        uz[s, 1] = jnp.concatenate(dy_rows, axis=0).astype(BF16)

    def send_unit(to):
        send(uz.at[lax.div(to, NZ)], g.at[:, x, zh, c, zl], z_sem.at[ring], along_z(to))

    for to in across[1:] + mates:
        send_unit(to)
    pl.semaphore_wait(vouch, 1)
    send_unit(across[0])
    g[:, x, zh, c, zl] = uz[zh]

    def unit(src):
        return g.at[:, x, lax.div(src, NZ), c, lax.rem(src, NZ)]

    quads = [lax.rem(q + k, RING // QUAD) for k in (0, 1, 3, 2)]

    def span(n):
        return lax.div(quads[n], NS), pl.ds(QUAD * lax.rem(quads[n], NS), QUAD)

    def pass_on(src):
        arrived(unit(src), z_sem.at[src])
        for to in mates:
            send(unit(src), unit(src), z_sem.at[src], along_z(to))

    def fan(ref, n):
        for i in range(NX - 1):
            send(ref(x), ref(x), x_sem.at[i, n], dev_peers[i])

    def unit_of(src):
        s, z = lax.div(src, NZ), lax.rem(src, NZ)
        return lambda xi: g.at[:, xi, s, c, z]

    def quad_of(n, cc):
        s, zs = span(n)
        return lambda xi: g.at[:, xi, s, cc, zs]

    nq = RING // QUAD
    groups = [quad_of(0, c)]
    for src in mates:
        arrived(unit(src), z_sem.at[src])
    fan(groups[0], 0)

    def forward(src):
        fan(unit_of(src), len(groups))
        groups.append(unit_of(src))

    for src in (across[1], across[2], across[0]):
        pass_on(src)
        forward(src)
    for n in (1, 2, 3):
        for j in range(1, QUAD):
            src = QUAD * quads[n] + lax.rem(ring + j, QUAD)
            arrived(unit(src), z_sem.at[src])
            forward(src)

    sources = [peers[1], peers[0], peers[2]]
    for n in range(nq):
        s, zs = span(n)
        members = {0: [0], 1: [1, 4, 5, 6], 2: [2, 7, 8, 9], 3: [3, 10, 11, 12]}[n]
        for m in members:
            for i in range(NX - 1):
                arrived(groups[m](sources[i]), x_sem.at[i, m])
        whole = g.at[:, :, s, c, zs]
        send(whole, whole, c_sem.at[n], dev_sib)

    for copy in loads:
        copy.wait()
    for n in range(nq):
        s, zs = span(n)
        arrived(g.at[:, :, s, other, zs], c_sem.at[n])

    def cols(xi, s):
        start = (s * NX + xi) * feat
        return slice(start, start + feat)

    def rows_of(a, xi, s):
        return g[a, xi, s].reshape(rows, feat)

    slices = [(xi, s) for xi in range(NX) for s in range(NS)]
    pre_gate = sum(dot_cols(rows_of(0, *i), wg[:, cols(*i)]) for i in slices)
    pre_up = sum(dot_cols(rows_of(0, *i), wu[:, cols(*i)]) for i in slices)
    grad_hidden = sum(dot_cols(rows_of(1, *i), wd[:, cols(*i)]) for i in slices)
    sig = jax.nn.sigmoid(pre_gate)
    silu = pre_gate * sig
    hid[0] = (silu * pre_up).astype(BF16)
    hid[1] = (grad_hidden * pre_up * sig * (1.0 + pre_gate * (1.0 - sig))).astype(BF16)
    hid[2] = (grad_hidden * silu).astype(BF16)

    for xi, s in slices:
        y0 = dot(hid[0], wd[:, cols(xi, s)])
        y1 = dot(hid[1], wg[:, cols(xi, s)]) + dot(hid[2], wu[:, cols(xi, s)])
        part[0, xi, s] = y0.astype(BF16).reshape(NC, NZ, ROWS, feat)
        part[1, xi, s] = y1.astype(BF16).reshape(NC, NZ, ROWS, feat)
    for n in reversed(range(nq)):
        s, zs = span(n)
        send(part.at[:, :, s, other, zs], sib.at[:, :, s, zs], s_sem.at[n], dev_sib)

    def chip_sum(xi, s, zs):
        return part[:, xi, s, c, zs].astype(F32) + sib[:, xi, s, zs].astype(F32)

    for n in reversed(range(nq)):
        s, zs = span(n)
        arrived(sib.at[:, :, s, zs], s_sem.at[n])
        for i in (2, 0, 1):
            xi = peers[i]
            part[:, xi, s, c, zs] = chip_sum(xi, s, zs).astype(BF16)
            send(part.at[:, xi, s, c, zs], xr.at[i, :, s, zs], r_sem.at[i, n], dev_peers[i])

    for xi, s in slices:
        gd[:, cols(xi, s)] = dot_rows(hid[0], rows_of(1, xi, s)).astype(BF16)
        gg[:, cols(xi, s)] = dot_rows(hid[1], rows_of(0, xi, s)).astype(BF16)
        gu[:, cols(xi, s)] = dot_rows(hid[2], rows_of(0, xi, s)).astype(BF16)
    stores = []
    for n, (vmem, hbm) in enumerate(((gd, gd_hbm), (gg, gg_hbm), (gu, gu_hbm))):
        copy = pltpu.make_async_copy(vmem, hbm.at[0], o_sem.at[n])
        copy.start()
        stores.append(copy)

    for n in reversed(range(nq)):
        s, zs = span(n)
        total = chip_sum(x, s, zs)
        for i in range(NX - 1):
            arrived(xr.at[i, :, s, zs], r_sem.at[i, n])
            total = total + xr[i, :, s, zs].astype(F32)
        for a in range(2):
            zbuf[pl.ds(QUAD * quads[n], QUAD), a] = total[a].astype(BF16)
        for j in range(QUAD):
            if n == 0:
                if j == 0:
                    continue
                to = QUAD * q + lax.rem(ring + j, QUAD)
            else:
                to = QUAD * quads[n] + j
            send(zbuf.at[to], rz.at[ring], q_sem.at[ring], along_z(to))
    rz[ring] = zbuf[ring]
    for src in around:
        arrived(rz.at[src], q_sem.at[src])

    for s in range(NS):
        total = rz[s * NZ].astype(F32)
        for z in range(1, NZ):
            total = total + rz[s * NZ + z].astype(F32)
        total = total.astype(BF16).astype(F32)
        block = slice(2 * CAP * s, 2 * CAP * (s + 1))
        for i in range(2):
            out_rows = total[0, 8 * i : 8 * i + 8]
            grad_rows = total[1, 8 * i : 8 * i + 8]
            snd2[2 * i, block] = jnp.where(sub, out_rows, pltpu.roll(grad_rows, CAP, 0))
            snd2[2 * i + 1, block] = jnp.where(sub, pltpu.roll(out_rows, CAP, 0), grad_rows)

    def return_copy(i):
        return pltpu.make_async_remote_copy(
            src_ref=snd2.at[i],
            dst_ref=rcv2.at[y],
            send_sem=f_sem.at[0, i],
            recv_sem=f_sem.at[1, y],
            device_id=device(jnp.int32(i), x, c),
            device_id_type=MESH,
        )

    for i in range(NX):
        mine = jnp.logical_and(diagonal, x == i)

        @pl.when(mine)
        def _():
            rcv2[y] = snd2[i]

        @pl.when(jnp.logical_not(mine))
        def _():
            return_copy(i).start()

    for i in range(NY):

        @pl.when(jnp.logical_not(jnp.logical_and(diagonal, y == i)))
        def _():
            arrived(rcv2.at[i], f_sem.at[1, i])

    home = rcv2[...].reshape(picks, feat)
    out_pick = jnp.where(first[:, :toks], both, 0.0)
    mixed_ref[...] = lax.dot_general(
        out_pick,
        gate * home,
        (((0,), (0,)), ((), ())),
        precision=lax.Precision.HIGHEST,
        preferred_element_type=F32,
    ).astype(BF16)
    grad_pick = (both - out_pick).astype(BF16)
    gtok_ref[...] = dot_rows(grad_pick, home.astype(BF16)).astype(BF16)

    for copy in stores:
        copy.wait()
    for copy in sent:
        copy.wait_send()
    for i in range(NY):

        @pl.when(jnp.logical_not(jnp.logical_and(diagonal, y == i)))
        def _():
            dispatch_copy(i).wait_send()

        @pl.when(jnp.logical_not(jnp.logical_and(diagonal, x == i)))
        def _():
            return_copy(i).wait_send()


def store_kernel(n, *refs):
    ins, outs, bufs, (sems,) = refs[:n], refs[n : 2 * n], refs[2 * n : 3 * n], refs[3 * n :]
    loads = [pltpu.make_async_copy(ins[i], bufs[i], sems.at[0, i]) for i in range(n)]
    stores = [pltpu.make_async_copy(bufs[i], outs[i], sems.at[1, i]) for i in range(n)]
    for copy in loads:
        copy.start()
    for load, store in zip(loads, stores):
        load.wait()
        store.start()
    for copy in stores:
        copy.wait()


def per_device(tokens, cotangent, route, gates, w_gate, w_up, w_down):
    assert lax.axis_size("dp") == NZ * NX * NC and lax.axis_size("expert") == NS * NY
    feat = tokens.shape[1]
    hidden = w_gate.shape[1]
    rows = NC * NZ * ROWS
    dma = pltpu.SemaphoreType.DMA
    vmem = pl.BlockSpec(memory_space=pltpu.VMEM)
    hbm = pl.BlockSpec(memory_space=pl.ANY)
    outs = (jax.ShapeDtypeStruct(tokens.shape, BF16),) * 2
    outs += (jax.ShapeDtypeStruct(w_gate.shape, BF16),) * 3
    nq = RING // QUAD
    results = pl.pallas_call(
        layer_kernel,
        out_shape=outs,
        in_specs=[vmem] * 4 + [hbm] * 3,
        out_specs=(vmem, vmem, hbm, hbm, hbm),
        scratch_shapes=[
            pltpu.VMEM((NY, NS * 2 * CAP, feat), F32),
            pltpu.VMEM((NX, NS * 2 * CAP, feat), F32),
            pltpu.VMEM((NS, 2, ROWS, feat), BF16),
            pltpu.VMEM((2, NX, NS, NC, NZ, ROWS, feat), BF16),
            pltpu.VMEM(w_gate.shape[1:], BF16),
            pltpu.VMEM(w_gate.shape[1:], BF16),
            pltpu.VMEM(w_gate.shape[1:], BF16),
            pltpu.VMEM((3, rows, hidden), BF16),
            pltpu.VMEM((2, NX, NS, NC, NZ, ROWS, feat), BF16),
            pltpu.VMEM((2, NX, NS, NZ, ROWS, feat), BF16),
            pltpu.VMEM((NX - 1, 2, NS, NZ, ROWS, feat), BF16),
            pltpu.VMEM((RING, 2, ROWS, feat), BF16),
            pltpu.VMEM((RING, 2, ROWS, feat), BF16),
            pltpu.VMEM((NX, NS * 2 * CAP, feat), F32),
            pltpu.VMEM((NY, NS * 2 * CAP, feat), F32),
            pltpu.VMEM(w_gate.shape[1:], BF16),
            pltpu.VMEM(w_gate.shape[1:], BF16),
            pltpu.VMEM(w_gate.shape[1:], BF16),
            dma((3,)),
            dma((3,)),
            dma((96,)),
            dma((2, NY)),
            dma((RING,)),
            dma((NX - 1, 13)),
            dma((nq,)),
            dma((nq,)),
            dma((NX - 1, nq)),
            dma((RING,)),
            dma((2, NY)),
            pltpu.SemaphoreType.REGULAR,
        ],
        compiler_params=pltpu.CompilerParams(
            collective_id=0, has_side_effects=True, vmem_limit_bytes=62 << 20
        ),
        name="expert_layer",
    )(tokens, cotangent, route.T, gates.T, w_gate, w_up, w_down)
    return pl.pallas_call(
        functools.partial(store_kernel, len(outs)),
        out_shape=outs,
        in_specs=[hbm] * len(outs),
        out_specs=(hbm,) * len(outs),
        scratch_shapes=[pltpu.VMEM(out.shape, out.dtype) for out in outs] + [dma((2, len(outs)))],
        compiler_params=pltpu.CompilerParams(vmem_limit_bytes=62 << 20),
        name="store_results",
    )(*results)


def solution(mesh):
    return jax.shard_map(
        per_device,
        mesh=mesh,
        in_specs=(
            P("dp", "expert"),
            P("dp", "expert"),
            P("dp", None),
            P("dp", None),
            P("expert", "dp", None),
            P("expert", "dp", None),
            P("expert", "dp", None),
        ),
        out_specs=(
            P("dp", "expert"),
            P("dp", "expert"),
            P("expert", "dp", None),
            P("expert", "dp", None),
            P("expert", "dp", None),
        ),
        check_vma=False,
    )
```

```python
import functools

import jax
import jax.numpy as jnp
from jax import lax
from jax.experimental import pallas as pl
from jax.experimental.pallas import tpu as pltpu
from jax.sharding import PartitionSpec as P

MESH = pl.DeviceIdType.MESH
BF16 = jnp.bfloat16
F32 = jnp.float32
NX = 4
NC = 2
NY = 4
NS = 2
NZ = 8
RING = NS * NZ
CAP = 4
ROWS = NX * CAP
QUAD = 4
PIECES = 4


def dot(left, right):
    return jnp.dot(left, right, preferred_element_type=F32)


def dot_cols(left, right):
    return lax.dot_general(left, right, (((1,), (1,)), ((), ())), preferred_element_type=F32)


def dot_rows(left, right):
    return lax.dot_general(left, right, (((0,), (0,)), ((), ())), preferred_element_type=F32)


def layer_kernel(
    tok_hbm,
    cot_hbm,
    route_hbm,
    gates_hbm,
    wg_hbm,
    wu_hbm,
    wd_hbm,
    mixed_ref,
    gtok_ref,
    gg_hbm,
    gu_hbm,
    gd_hbm,
    tok_ref,
    cot_ref,
    route_ref,
    gates_ref,
    snd,
    rcv,
    uz,
    g,
    wg,
    wu,
    wd,
    hid,
    part,
    sib,
    xr,
    zbuf,
    rz,
    snd2,
    rcv2,
    gg,
    gu,
    gd,
    i_sem,
    w_sem,
    o_sem,
    send_sem,
    d_sem,
    z_sem,
    x_sem,
    c_sem,
    s_sem,
    r_sem,
    q_sem,
    f_sem,
    vouch,
):
    p = lax.axis_index("dp")
    e = lax.axis_index("expert")
    zl = lax.div(p, NX * NC)
    x = lax.rem(lax.div(p, NC), NX)
    c = lax.rem(p, NC)
    zh = lax.div(e, NY)
    y = lax.rem(e, NY)
    ring = zh * NZ + zl
    other = 1 - c
    rows = NC * NZ * ROWS
    toks, feat = tok_ref.shape
    peers = [lax.rem(x + k, NX) for k in (1, 3, 2)]

    def device(xx, yy, cc):
        return (zl * (NX * NC) + xx * NC + cc, zh * NY + yy)

    def along_z(to):
        low = lax.rem(to, NZ)
        return (low * (NX * NC) + x * NC + c, lax.div(to, NZ) * NY + y)

    dev_peers = [device(xx, y, c) for xx in peers]
    dev_sib = device(x, y, other)
    sent = []

    def send(src, dst, rsem, to):
        copy = pltpu.make_async_remote_copy(
            src_ref=src,
            dst_ref=dst,
            send_sem=send_sem.at[len(sent)],
            recv_sem=rsem,
            device_id=to,
            device_id_type=MESH,
        )
        copy.start()
        sent.append(copy)

    def arrived(dst, rsem):
        pltpu.make_async_remote_copy(
            src_ref=dst,
            dst_ref=dst,
            send_sem=send_sem.at[0],
            recv_sem=rsem,
            device_id=dev_sib,
            device_id_type=MESH,
        ).wait_recv()

    barrier = pltpu.get_barrier_semaphore()

    def greet(to):
        pl.semaphore_signal(barrier, inc=1, device_id=to, device_id_type=MESH)

    around = [lax.rem(ring + k, RING) for k in range(1, RING)]
    q = lax.div(ring, QUAD)
    mates = [QUAD * q + lax.rem(ring + j, QUAD) for j in range(1, QUAD)]
    across = [lax.rem(ring + k * QUAD, RING) for k in (2, 1, 3)]
    for to in across[1:] + mates:
        greet(along_z(to))
    diagonal = x == y
    for i in range(NY):

        @pl.when(jnp.logical_not(jnp.logical_and(diagonal, y == i)))
        def _():
            greet(device(y, jnp.int32(i), c))

        @pl.when(jnp.logical_not(jnp.logical_and(diagonal, x == i)))
        def _():
            greet(device(jnp.int32(i), x, c))

    for to in dev_peers:
        greet(to)
    greet(dev_sib)

    tables = [
        pltpu.make_async_copy(hbm, vmem, i_sem.at[n])
        for n, (hbm, vmem) in enumerate(
            (
                (route_hbm, route_ref),
                (gates_hbm, gates_ref),
                (tok_hbm, tok_ref),
                (cot_hbm, cot_ref),
            )
        )
    ]
    for copy in tables:
        copy.start()
    loads = []
    for n, (hbm, vmem) in enumerate(((wg_hbm, wg), (wu_hbm, wu), (wd_hbm, wd))):
        copy = pltpu.make_async_copy(hbm.at[0], vmem, w_sem.at[n])
        copy.start()
        loads.append(copy)

    for copy in tables:
        copy.wait()

    picks = NY * NS * 2 * CAP
    row = lax.broadcasted_iota(jnp.int32, (picks, toks), 0)
    row_e = ((row >> 3) & 1) * NY + (row >> 4)
    row_c = (row & 3).astype(F32)
    m0 = (route_ref[0:1, :] == row_e).astype(F32)
    m1 = (route_ref[1:2, :] == row_e).astype(F32)
    earlier = (
        lax.broadcasted_iota(jnp.int32, (toks, toks), 0)
        < lax.broadcasted_iota(jnp.int32, (toks, toks), 1)
    ).astype(F32)
    before = dot(m0 + m1, earlier)
    p0 = jnp.where(before == row_c, m0, 0.0)
    p1 = jnp.where(before + m0 == row_c, m1, 0.0)
    both = p0 + p1
    gate = jnp.sum(p0 * gates_ref[0:1, :] + p1 * gates_ref[1:2, :], axis=1, keepdims=True)
    first = ((lax.broadcasted_iota(jnp.int32, (picks, feat), 0) >> 2) & 1) == 0
    pick = both.astype(BF16)
    placed_grad = (gate * dot(pick, cot_ref[...])).astype(BF16).astype(F32)
    placed = jnp.where(first, dot(pick, tok_ref[...]), placed_grad)
    snd[...] = placed.reshape(NY, NS * 2 * CAP, feat)

    near = jnp.where(diagonal, 2 * NY - 2, 2 * NY)
    pl.semaphore_wait(barrier, near + 2 + (QUAD - 1) + (NX - 1) + 1)

    pl.semaphore_signal(vouch, inc=1, device_id=along_z(across[2]), device_id_type=MESH)

    def dispatch_copy(i):
        return pltpu.make_async_remote_copy(
            src_ref=snd.at[i],
            dst_ref=rcv.at[x],
            send_sem=d_sem.at[0, i],
            recv_sem=d_sem.at[1, x],
            device_id=device(y, jnp.int32(i), c),
            device_id_type=MESH,
        )

    for i in range(NY):
        mine = jnp.logical_and(diagonal, y == i)

        @pl.when(mine)
        def _():
            rcv[x] = snd[i]

        @pl.when(jnp.logical_not(mine))
        def _():
            dispatch_copy(i).start()

    for i in range(NX):

        @pl.when(jnp.logical_not(jnp.logical_and(diagonal, x == i)))
        def _():
            arrived(rcv.at[i], d_sem.at[1, i])

    sub = lax.broadcasted_iota(jnp.int32, (2 * CAP, feat), 0) < CAP
    for s in range(NS):
        t = [rcv[i, 2 * CAP * s : 2 * CAP * (s + 1)] for i in range(NX)]
        r = [pltpu.roll(v, CAP, 0) for v in t]
        xs_rows = [jnp.where(sub, t[0], r[1]), jnp.where(sub, t[2], r[3])]
        dy_rows = [jnp.where(sub, r[0], t[1]), jnp.where(sub, r[2], t[3])]
        uz[s, 0] = jnp.concatenate(xs_rows, axis=0).astype(BF16)
        uz[s, 1] = jnp.concatenate(dy_rows, axis=0).astype(BF16)

    def send_unit(to):
        send(uz.at[lax.div(to, NZ)], g.at[:, x, zh, c, zl], z_sem.at[ring], along_z(to))

    for to in across[1:] + mates:
        send_unit(to)
    pl.semaphore_wait(vouch, 1)
    send_unit(across[0])
    g[:, x, zh, c, zl] = uz[zh]

    def unit(src):
        return g.at[:, x, lax.div(src, NZ), c, lax.rem(src, NZ)]

    quads = [lax.rem(q + k, RING // QUAD) for k in (0, 1, 3, 2)]

    def span(n):
        return lax.div(quads[n], NS), pl.ds(QUAD * lax.rem(quads[n], NS), QUAD)

    def pass_on(src):
        arrived(unit(src), z_sem.at[src])
        for to in mates:
            send(unit(src), unit(src), z_sem.at[src], along_z(to))

    def fan(ref, n):
        for i in range(NX - 1):
            send(ref(x), ref(x), x_sem.at[i, n], dev_peers[i])

    def unit_of(src):
        s, z = lax.div(src, NZ), lax.rem(src, NZ)
        return lambda xi: g.at[:, xi, s, c, z]

    def quad_of(n, cc):
        s, zs = span(n)
        return lambda xi: g.at[:, xi, s, cc, zs]

    nq = RING // QUAD
    groups = [quad_of(0, c)]
    for src in mates:
        arrived(unit(src), z_sem.at[src])
    fan(groups[0], 0)

    def forward(src):
        fan(unit_of(src), len(groups))
        groups.append(unit_of(src))

    for src in (across[1], across[2], across[0]):
        pass_on(src)
        forward(src)
    for n in (1, 2, 3):
        for j in range(1, QUAD):
            src = QUAD * quads[n] + lax.rem(ring + j, QUAD)
            arrived(unit(src), z_sem.at[src])
            forward(src)

    sources = [peers[1], peers[0], peers[2]]
    for n in range(nq):
        s, zs = span(n)
        members = {0: [0], 1: [1, 4, 5, 6], 2: [2, 7, 8, 9], 3: [3, 10, 11, 12]}[n]
        for m in members:
            for i in range(NX - 1):
                arrived(groups[m](sources[i]), x_sem.at[i, m])
        whole = g.at[:, :, s, c, zs]
        send(whole, whole, c_sem.at[n], dev_sib)

    for copy in loads:
        copy.wait()
    for n in range(nq):
        s, zs = span(n)
        arrived(g.at[:, :, s, other, zs], c_sem.at[n])

    def cols(xi, s):
        start = (s * NX + xi) * feat
        return slice(start, start + feat)

    def rows_of(a, xi, s):
        return g[a, xi, s].reshape(rows, feat)

    slices = [(xi, s) for xi in range(NX) for s in range(NS)]
    pre_gate = sum(dot_cols(rows_of(0, *i), wg[:, cols(*i)]) for i in slices)
    pre_up = sum(dot_cols(rows_of(0, *i), wu[:, cols(*i)]) for i in slices)
    grad_hidden = sum(dot_cols(rows_of(1, *i), wd[:, cols(*i)]) for i in slices)
    sig = jax.nn.sigmoid(pre_gate)
    silu = pre_gate * sig
    hid[0] = (silu * pre_up).astype(BF16)
    hid[1] = (grad_hidden * pre_up * sig * (1.0 + pre_gate * (1.0 - sig))).astype(BF16)
    hid[2] = (grad_hidden * silu).astype(BF16)

    for xi, s in slices:
        y0 = dot(hid[0], wd[:, cols(xi, s)])
        y1 = dot(hid[1], wg[:, cols(xi, s)]) + dot(hid[2], wu[:, cols(xi, s)])
        part[0, xi, s] = y0.astype(BF16).reshape(NC, NZ, ROWS, feat)
        part[1, xi, s] = y1.astype(BF16).reshape(NC, NZ, ROWS, feat)
    for n in reversed(range(nq)):
        s, zs = span(n)
        send(part.at[:, :, s, other, zs], sib.at[:, :, s, zs], s_sem.at[n], dev_sib)

    def chip_sum(xi, s, zs):
        return part[:, xi, s, c, zs].astype(F32) + sib[:, xi, s, zs].astype(F32)

    for n in reversed(range(nq)):
        s, zs = span(n)
        arrived(sib.at[:, :, s, zs], s_sem.at[n])
        for i in (2, 0, 1):
            xi = peers[i]
            part[:, xi, s, c, zs] = chip_sum(xi, s, zs).astype(BF16)
            send(part.at[:, xi, s, c, zs], xr.at[i, :, s, zs], r_sem.at[i, n], dev_peers[i])

    stores = []

    def weight_grad(k, a, out, hbm):
        across_rows = hid[k].astype(F32).T.astype(BF16)
        for xi, s in slices:
            out[:, cols(xi, s)] = dot(across_rows, rows_of(a, xi, s)).astype(BF16)
        copy = pltpu.make_async_copy(out, hbm.at[0], o_sem.at[k])
        copy.start()
        stores.append(copy)

    weight_grad(0, 1, gd, gd_hbm)

    for n in reversed(range(nq)):
        s, zs = span(n)
        total = chip_sum(x, s, zs)
        for i in range(NX - 1):
            arrived(xr.at[i, :, s, zs], r_sem.at[i, n])
            total = total + xr[i, :, s, zs].astype(F32)
        for a in range(2):
            zbuf[pl.ds(QUAD * quads[n], QUAD), a] = total[a].astype(BF16)
        for j in range(QUAD):
            if n == 0:
                if j == 0:
                    continue
                to = QUAD * q + lax.rem(ring + j, QUAD)
            else:
                to = QUAD * quads[n] + j
            send(zbuf.at[to], rz.at[ring], q_sem.at[ring], along_z(to))
    rz[ring] = zbuf[ring]
    weight_grad(1, 0, gg, gg_hbm)
    weight_grad(2, 0, gu, gu_hbm)
    for src in around:
        arrived(rz.at[src], q_sem.at[src])

    for s in range(NS):
        total = rz[s * NZ].astype(F32)
        for z in range(1, NZ):
            total = total + rz[s * NZ + z].astype(F32)
        total = total.astype(BF16).astype(F32)
        block = slice(2 * CAP * s, 2 * CAP * (s + 1))
        for i in range(2):
            out_rows = total[0, 8 * i : 8 * i + 8]
            grad_rows = total[1, 8 * i : 8 * i + 8]
            snd2[2 * i, block] = jnp.where(sub, out_rows, pltpu.roll(grad_rows, CAP, 0))
            snd2[2 * i + 1, block] = jnp.where(sub, pltpu.roll(out_rows, CAP, 0), grad_rows)

    def return_copy(i):
        return pltpu.make_async_remote_copy(
            src_ref=snd2.at[i],
            dst_ref=rcv2.at[y],
            send_sem=f_sem.at[0, i],
            recv_sem=f_sem.at[1, y],
            device_id=device(jnp.int32(i), x, c),
            device_id_type=MESH,
        )

    for i in range(NX):
        mine = jnp.logical_and(diagonal, x == i)

        @pl.when(mine)
        def _():
            rcv2[y] = snd2[i]

        @pl.when(jnp.logical_not(mine))
        def _():
            return_copy(i).start()

    for i in range(NY):

        @pl.when(jnp.logical_not(jnp.logical_and(diagonal, y == i)))
        def _():
            arrived(rcv2.at[i], f_sem.at[1, i])

    home = rcv2[...].reshape(picks, feat)
    out_pick = jnp.where(first[:, :toks], both, 0.0)
    mixed_ref[...] = lax.dot_general(
        out_pick,
        gate * home,
        (((0,), (0,)), ((), ())),
        precision=lax.Precision.HIGHEST,
        preferred_element_type=F32,
    ).astype(BF16)
    grad_pick = (both - out_pick).astype(BF16)
    gtok_ref[...] = dot_rows(grad_pick, home.astype(BF16)).astype(BF16)

    for copy in stores:
        copy.wait()
    for copy in sent:
        copy.wait_send()
    for i in range(NY):

        @pl.when(jnp.logical_not(jnp.logical_and(diagonal, y == i)))
        def _():
            dispatch_copy(i).wait_send()

        @pl.when(jnp.logical_not(jnp.logical_and(diagonal, x == i)))
        def _():
            return_copy(i).wait_send()


def store_kernel(n, *refs):
    ins, outs, bufs, (sems,) = refs[:n], refs[n : 2 * n], refs[2 * n : 3 * n], refs[3 * n :]
    loads, stores = [], []
    for i in range(n):
        shape = ins[i].shape
        for j in range(PIECES if len(shape) == 3 else 1):
            k = len(loads)
            if len(shape) == 3:
                rows = shape[1] // PIECES
                at = (0, pl.ds(j * rows, rows))
            else:
                at = (slice(None),)
            loads.append(pltpu.make_async_copy(ins[i].at[at], bufs[i].at[at], sems.at[0, k]))
            stores.append(pltpu.make_async_copy(bufs[i].at[at], outs[i].at[at], sems.at[1, k]))
    for copy in loads:
        copy.start()
    for load, store in zip(loads, stores):
        load.wait()
        store.start()
    for copy in stores:
        copy.wait()


def per_device(tokens, cotangent, route, gates, w_gate, w_up, w_down):
    assert lax.axis_size("dp") == NZ * NX * NC and lax.axis_size("expert") == NS * NY
    feat = tokens.shape[1]
    hidden = w_gate.shape[1]
    rows = NC * NZ * ROWS
    dma = pltpu.SemaphoreType.DMA
    vmem = pl.BlockSpec(memory_space=pltpu.VMEM)
    hbm = pl.BlockSpec(memory_space=pl.ANY)
    outs = (jax.ShapeDtypeStruct(tokens.shape, BF16),) * 2
    outs += (jax.ShapeDtypeStruct(w_gate.shape, BF16),) * 3
    nq = RING // QUAD
    results = pl.pallas_call(
        layer_kernel,
        out_shape=outs,
        in_specs=[hbm] * 7,
        out_specs=(vmem, vmem, hbm, hbm, hbm),
        scratch_shapes=[
            pltpu.VMEM(tokens.shape, BF16),
            pltpu.VMEM(tokens.shape, BF16),
            pltpu.VMEM(route.shape[::-1], route.dtype),
            pltpu.VMEM(route.shape[::-1], gates.dtype),
            pltpu.VMEM((NY, NS * 2 * CAP, feat), F32),
            pltpu.VMEM((NX, NS * 2 * CAP, feat), F32),
            pltpu.VMEM((NS, 2, ROWS, feat), BF16),
            pltpu.VMEM((2, NX, NS, NC, NZ, ROWS, feat), BF16),
            pltpu.VMEM(w_gate.shape[1:], BF16),
            pltpu.VMEM(w_gate.shape[1:], BF16),
            pltpu.VMEM(w_gate.shape[1:], BF16),
            pltpu.VMEM((3, rows, hidden), BF16),
            pltpu.VMEM((2, NX, NS, NC, NZ, ROWS, feat), BF16),
            pltpu.VMEM((2, NX, NS, NZ, ROWS, feat), BF16),
            pltpu.VMEM((NX - 1, 2, NS, NZ, ROWS, feat), BF16),
            pltpu.VMEM((RING, 2, ROWS, feat), BF16),
            pltpu.VMEM((RING, 2, ROWS, feat), BF16),
            pltpu.VMEM((NX, NS * 2 * CAP, feat), F32),
            pltpu.VMEM((NY, NS * 2 * CAP, feat), F32),
            pltpu.VMEM(w_gate.shape[1:], BF16),
            pltpu.VMEM(w_gate.shape[1:], BF16),
            pltpu.VMEM(w_gate.shape[1:], BF16),
            dma((4,)),
            dma((3,)),
            dma((3,)),
            dma((96,)),
            dma((2, NY)),
            dma((RING,)),
            dma((NX - 1, 13)),
            dma((nq,)),
            dma((nq,)),
            dma((NX - 1, nq)),
            dma((RING,)),
            dma((2, NY)),
            pltpu.SemaphoreType.REGULAR,
        ],
        compiler_params=pltpu.CompilerParams(
            collective_id=0, has_side_effects=True, vmem_limit_bytes=62 << 20
        ),
        name="expert_layer",
    )(tokens, cotangent, route.T, gates.T, w_gate, w_up, w_down)
    return pl.pallas_call(
        functools.partial(store_kernel, len(outs)),
        out_shape=outs,
        in_specs=[hbm] * len(outs),
        out_specs=(hbm,) * len(outs),
        scratch_shapes=[pltpu.VMEM(out.shape, out.dtype) for out in outs] + [dma((2, 3 * PIECES + 2))],
        compiler_params=pltpu.CompilerParams(vmem_limit_bytes=62 << 20),
        name="store_results",
    )(*results)


def solution(mesh):
    return jax.shard_map(
        per_device,
        mesh=mesh,
        in_specs=(
            P("dp", "expert"),
            P("dp", "expert"),
            P("dp", None),
            P("dp", None),
            P("expert", "dp", None),
            P("expert", "dp", None),
            P("expert", "dp", None),
        ),
        out_specs=(
            P("dp", "expert"),
            P("dp", "expert"),
            P("expert", "dp", None),
            P("expert", "dp", None),
            P("expert", "dp", None),
        ),
        check_vma=False,
    )
```

```python
import functools

import jax
import jax.numpy as jnp
from jax import lax
from jax.experimental import pallas as pl
from jax.experimental.pallas import tpu as pltpu
from jax.sharding import PartitionSpec as P

MESH = pl.DeviceIdType.MESH
BF16 = jnp.bfloat16
F32 = jnp.float32
NX = 4
NC = 2
NY = 4
NS = 2
NZ = 8
RING = NS * NZ
CAP = 4
ROWS = NX * CAP
QUAD = 4
PIECES = 4


def dot(left, right):
    return jnp.dot(left, right, preferred_element_type=F32)


def dot_cols(left, right):
    return lax.dot_general(left, right, (((1,), (1,)), ((), ())), preferred_element_type=F32)


def dot_rows(left, right):
    return lax.dot_general(left, right, (((0,), (0,)), ((), ())), preferred_element_type=F32)


def layer_kernel(
    tok_hbm,
    cot_hbm,
    route_hbm,
    gates_hbm,
    wg_hbm,
    wu_hbm,
    wd_hbm,
    mixed_hbm,
    gtok_hbm,
    gg_hbm,
    gu_hbm,
    gd_hbm,
    tok_ref,
    cot_ref,
    route_ref,
    gates_ref,
    mixed_ref,
    gtok_ref,
    snd,
    rcv,
    uz,
    g,
    wg,
    wu,
    wd,
    hid,
    part,
    sib,
    xr,
    zbuf,
    rz,
    snd2,
    rcv2,
    gg,
    gu,
    gd,
    i_sem,
    w_sem,
    o_sem,
    send_sem,
    d_sem,
    z_sem,
    x_sem,
    c_sem,
    s_sem,
    r_sem,
    q_sem,
    f_sem,
    vouch,
):
    p = lax.axis_index("dp")
    e = lax.axis_index("expert")
    zl = lax.div(p, NX * NC)
    x = lax.rem(lax.div(p, NC), NX)
    c = lax.rem(p, NC)
    zh = lax.div(e, NY)
    y = lax.rem(e, NY)
    ring = zh * NZ + zl
    other = 1 - c
    rows = NC * NZ * ROWS
    toks, feat = tok_ref.shape
    peers = [lax.rem(x + k, NX) for k in (1, 3, 2)]

    def device(xx, yy, cc):
        return (zl * (NX * NC) + xx * NC + cc, zh * NY + yy)

    def along_z(to):
        low = lax.rem(to, NZ)
        return (low * (NX * NC) + x * NC + c, lax.div(to, NZ) * NY + y)

    dev_peers = [device(xx, y, c) for xx in peers]
    dev_sib = device(x, y, other)
    sent = []

    def send(src, dst, rsem, to):
        copy = pltpu.make_async_remote_copy(
            src_ref=src,
            dst_ref=dst,
            send_sem=send_sem.at[len(sent)],
            recv_sem=rsem,
            device_id=to,
            device_id_type=MESH,
        )
        copy.start()
        sent.append(copy)

    def arrived(dst, rsem):
        pltpu.make_async_remote_copy(
            src_ref=dst,
            dst_ref=dst,
            send_sem=send_sem.at[0],
            recv_sem=rsem,
            device_id=dev_sib,
            device_id_type=MESH,
        ).wait_recv()

    barrier = pltpu.get_barrier_semaphore()

    def greet(to):
        pl.semaphore_signal(barrier, inc=1, device_id=to, device_id_type=MESH)

    around = [lax.rem(ring + k, RING) for k in range(1, RING)]
    q = lax.div(ring, QUAD)
    mates = [QUAD * q + lax.rem(ring + j, QUAD) for j in range(1, QUAD)]
    across = [lax.rem(ring + k * QUAD, RING) for k in (2, 1, 3)]
    for to in across[1:] + mates:
        greet(along_z(to))
    diagonal = x == y
    for i in range(NY):

        @pl.when(jnp.logical_not(jnp.logical_and(diagonal, y == i)))
        def _():
            greet(device(y, jnp.int32(i), c))

        @pl.when(jnp.logical_not(jnp.logical_and(diagonal, x == i)))
        def _():
            greet(device(jnp.int32(i), x, c))

    for to in dev_peers:
        greet(to)
    greet(dev_sib)

    tables = [
        pltpu.make_async_copy(hbm, vmem, i_sem.at[n])
        for n, (hbm, vmem) in enumerate(
            (
                (route_hbm, route_ref),
                (gates_hbm, gates_ref),
                (tok_hbm, tok_ref),
                (cot_hbm, cot_ref),
            )
        )
    ]
    for copy in tables:
        copy.start()
    loads = []
    for n, (hbm, vmem) in enumerate(((wg_hbm, wg), (wu_hbm, wu), (wd_hbm, wd))):
        copy = pltpu.make_async_copy(hbm.at[0], vmem, w_sem.at[n])
        copy.start()
        loads.append(copy)

    for copy in tables:
        copy.wait()

    picks = NY * NS * 2 * CAP
    row = lax.broadcasted_iota(jnp.int32, (picks, toks), 0)
    row_e = ((row >> 3) & 1) * NY + (row >> 4)
    row_c = (row & 3).astype(F32)
    m0 = (route_ref[0:1, :] == row_e).astype(F32)
    m1 = (route_ref[1:2, :] == row_e).astype(F32)
    earlier = (
        lax.broadcasted_iota(jnp.int32, (toks, toks), 0)
        < lax.broadcasted_iota(jnp.int32, (toks, toks), 1)
    ).astype(F32)
    before = dot(m0 + m1, earlier)
    p0 = jnp.where(before == row_c, m0, 0.0)
    p1 = jnp.where(before + m0 == row_c, m1, 0.0)
    both = p0 + p1
    gate = jnp.sum(p0 * gates_ref[0:1, :] + p1 * gates_ref[1:2, :], axis=1, keepdims=True)
    first = ((lax.broadcasted_iota(jnp.int32, (picks, feat), 0) >> 2) & 1) == 0
    pick = both.astype(BF16)
    placed_grad = (gate * dot(pick, cot_ref[...])).astype(BF16).astype(F32)
    placed = jnp.where(first, dot(pick, tok_ref[...]), placed_grad)
    snd[...] = placed.reshape(NY, NS * 2 * CAP, feat)

    near = jnp.where(diagonal, 2 * NY - 2, 2 * NY)
    pl.semaphore_wait(barrier, near + 2 + (QUAD - 1) + (NX - 1) + 1)

    pl.semaphore_signal(vouch, inc=1, device_id=along_z(across[2]), device_id_type=MESH)

    def dispatch_copy(i):
        return pltpu.make_async_remote_copy(
            src_ref=snd.at[i],
            dst_ref=rcv.at[x],
            send_sem=d_sem.at[0, i],
            recv_sem=d_sem.at[1, x],
            device_id=device(y, jnp.int32(i), c),
            device_id_type=MESH,
        )

    for i in range(NY):
        mine = jnp.logical_and(diagonal, y == i)

        @pl.when(mine)
        def _():
            rcv[x] = snd[i]

        @pl.when(jnp.logical_not(mine))
        def _():
            dispatch_copy(i).start()

    for i in range(NX):

        @pl.when(jnp.logical_not(jnp.logical_and(diagonal, x == i)))
        def _():
            arrived(rcv.at[i], d_sem.at[1, i])

    sub = lax.broadcasted_iota(jnp.int32, (2 * CAP, feat), 0) < CAP
    for s in range(NS):
        t = [rcv[i, 2 * CAP * s : 2 * CAP * (s + 1)] for i in range(NX)]
        r = [pltpu.roll(v, CAP, 0) for v in t]
        xs_rows = [jnp.where(sub, t[0], r[1]), jnp.where(sub, t[2], r[3])]
        dy_rows = [jnp.where(sub, r[0], t[1]), jnp.where(sub, r[2], t[3])]
        uz[s, 0] = jnp.concatenate(xs_rows, axis=0).astype(BF16)
        uz[s, 1] = jnp.concatenate(dy_rows, axis=0).astype(BF16)

    def send_unit(to):
        send(uz.at[lax.div(to, NZ)], g.at[:, x, zh, c, zl], z_sem.at[ring], along_z(to))

    for to in across[1:] + mates:
        send_unit(to)
    pl.semaphore_wait(vouch, 1)
    send_unit(across[0])
    g[:, x, zh, c, zl] = uz[zh]

    def unit(src):
        return g.at[:, x, lax.div(src, NZ), c, lax.rem(src, NZ)]

    quads = [lax.rem(q + k, RING // QUAD) for k in (0, 1, 3, 2)]

    def span(n):
        return lax.div(quads[n], NS), pl.ds(QUAD * lax.rem(quads[n], NS), QUAD)

    def pass_on(src):
        arrived(unit(src), z_sem.at[src])
        for to in mates:
            send(unit(src), unit(src), z_sem.at[src], along_z(to))

    def fan(ref, n):
        for i in range(NX - 1):
            send(ref(x), ref(x), x_sem.at[i, n], dev_peers[i])

    def unit_of(src):
        s, z = lax.div(src, NZ), lax.rem(src, NZ)
        return lambda xi: g.at[:, xi, s, c, z]

    def quad_of(n, cc):
        s, zs = span(n)
        return lambda xi: g.at[:, xi, s, cc, zs]

    nq = RING // QUAD
    groups = [quad_of(0, c)]
    for src in mates:
        arrived(unit(src), z_sem.at[src])
    fan(groups[0], 0)

    def forward(src):
        fan(unit_of(src), len(groups))
        groups.append(unit_of(src))

    for src in (across[1], across[2], across[0]):
        pass_on(src)
        forward(src)
    for n in (1, 2, 3):
        for j in range(1, QUAD):
            src = QUAD * quads[n] + lax.rem(ring + j, QUAD)
            arrived(unit(src), z_sem.at[src])
            forward(src)

    sources = [peers[1], peers[0], peers[2]]
    for n in range(nq):
        s, zs = span(n)
        members = {0: [0], 1: [1, 4, 5, 6], 2: [2, 7, 8, 9], 3: [3, 10, 11, 12]}[n]
        for m in members:
            for i in range(NX - 1):
                arrived(groups[m](sources[i]), x_sem.at[i, m])
        whole = g.at[:, :, s, c, zs]
        send(whole, whole, c_sem.at[n], dev_sib)

    for copy in loads:
        copy.wait()
    for n in range(nq):
        s, zs = span(n)
        arrived(g.at[:, :, s, other, zs], c_sem.at[n])

    def cols(xi, s):
        start = (s * NX + xi) * feat
        return slice(start, start + feat)

    def rows_of(a, xi, s):
        return g[a, xi, s].reshape(rows, feat)

    slices = [(xi, s) for xi in range(NX) for s in range(NS)]
    pre_gate = sum(dot_cols(rows_of(0, *i), wg[:, cols(*i)]) for i in slices)
    pre_up = sum(dot_cols(rows_of(0, *i), wu[:, cols(*i)]) for i in slices)
    grad_hidden = sum(dot_cols(rows_of(1, *i), wd[:, cols(*i)]) for i in slices)
    sig = jax.nn.sigmoid(pre_gate)
    silu = pre_gate * sig
    hid[0] = (silu * pre_up).astype(BF16)
    hid[1] = (grad_hidden * pre_up * sig * (1.0 + pre_gate * (1.0 - sig))).astype(BF16)
    hid[2] = (grad_hidden * silu).astype(BF16)

    for xi, s in slices:
        y0 = dot(hid[0], wd[:, cols(xi, s)])
        y1 = dot(hid[1], wg[:, cols(xi, s)]) + dot(hid[2], wu[:, cols(xi, s)])
        part[0, xi, s] = y0.astype(BF16).reshape(NC, NZ, ROWS, feat)
        part[1, xi, s] = y1.astype(BF16).reshape(NC, NZ, ROWS, feat)
    for n in reversed(range(nq)):
        s, zs = span(n)
        send(part.at[:, :, s, other, zs], sib.at[:, :, s, zs], s_sem.at[n], dev_sib)

    def chip_sum(xi, s, zs):
        return part[:, xi, s, c, zs].astype(F32) + sib[:, xi, s, zs].astype(F32)

    for n in reversed(range(nq)):
        s, zs = span(n)
        arrived(sib.at[:, :, s, zs], s_sem.at[n])
        for i in (2, 0, 1):
            xi = peers[i]
            part[:, xi, s, c, zs] = chip_sum(xi, s, zs).astype(BF16)
            send(part.at[:, xi, s, c, zs], xr.at[i, :, s, zs], r_sem.at[i, n], dev_peers[i])

    stores = []

    def weight_grad(k, a, out, hbm):
        across_rows = hid[k].astype(F32).T.astype(BF16)
        for xi, s in slices:
            out[:, cols(xi, s)] = dot(across_rows, rows_of(a, xi, s)).astype(BF16)
        copy = pltpu.make_async_copy(out, hbm.at[0], o_sem.at[k])
        copy.start()
        stores.append(copy)

    weight_grad(0, 1, gd, gd_hbm)

    for n in reversed(range(nq)):
        s, zs = span(n)
        total = chip_sum(x, s, zs)
        for i in range(NX - 1):
            arrived(xr.at[i, :, s, zs], r_sem.at[i, n])
            total = total + xr[i, :, s, zs].astype(F32)
        for a in range(2):
            zbuf[pl.ds(QUAD * quads[n], QUAD), a] = total[a].astype(BF16)
        for j in range(QUAD):
            if n == 0:
                if j == 0:
                    continue
                to = QUAD * q + lax.rem(ring + j, QUAD)
            else:
                to = QUAD * quads[n] + j
            send(zbuf.at[to], rz.at[ring], q_sem.at[ring], along_z(to))
    rz[ring] = zbuf[ring]
    weight_grad(1, 0, gg, gg_hbm)
    weight_grad(2, 0, gu, gu_hbm)
    for src in around:
        arrived(rz.at[src], q_sem.at[src])

    for s in range(NS):
        total = rz[s * NZ].astype(F32)
        for z in range(1, NZ):
            total = total + rz[s * NZ + z].astype(F32)
        total = total.astype(BF16).astype(F32)
        block = slice(2 * CAP * s, 2 * CAP * (s + 1))
        for i in range(2):
            out_rows = total[0, 8 * i : 8 * i + 8]
            grad_rows = total[1, 8 * i : 8 * i + 8]
            snd2[2 * i, block] = jnp.where(sub, out_rows, pltpu.roll(grad_rows, CAP, 0))
            snd2[2 * i + 1, block] = jnp.where(sub, pltpu.roll(out_rows, CAP, 0), grad_rows)

    def return_copy(i):
        return pltpu.make_async_remote_copy(
            src_ref=snd2.at[i],
            dst_ref=rcv2.at[y],
            send_sem=f_sem.at[0, i],
            recv_sem=f_sem.at[1, y],
            device_id=device(jnp.int32(i), x, c),
            device_id_type=MESH,
        )

    for i in range(NX):
        mine = jnp.logical_and(diagonal, x == i)

        @pl.when(mine)
        def _():
            rcv2[y] = snd2[i]

        @pl.when(jnp.logical_not(mine))
        def _():
            return_copy(i).start()

    for copy in sent:
        copy.wait_send()
    for i in range(NY):

        @pl.when(jnp.logical_not(jnp.logical_and(diagonal, y == i)))
        def _():
            arrived(rcv2.at[i], f_sem.at[1, i])

    home = rcv2[...].reshape(picks, feat)
    out_pick = jnp.where(first[:, :toks], both, 0.0)
    mixed_ref[...] = lax.dot_general(
        out_pick,
        gate * home,
        (((0,), (0,)), ((), ())),
        precision=lax.Precision.HIGHEST,
        preferred_element_type=F32,
    ).astype(BF16)
    grad_pick = (both - out_pick).astype(BF16)
    gtok_ref[...] = dot_rows(grad_pick, home.astype(BF16)).astype(BF16)
    for n, (vmem, hbm) in enumerate(((mixed_ref, mixed_hbm), (gtok_ref, gtok_hbm))):
        copy = pltpu.make_async_copy(vmem, hbm, o_sem.at[3 + n])
        copy.start()
        stores.append(copy)

    for copy in stores:
        copy.wait()
    for i in range(NY):

        @pl.when(jnp.logical_not(jnp.logical_and(diagonal, y == i)))
        def _():
            dispatch_copy(i).wait_send()

        @pl.when(jnp.logical_not(jnp.logical_and(diagonal, x == i)))
        def _():
            return_copy(i).wait_send()


def store_kernel(n, *refs):
    ins, outs, bufs, (sems,) = refs[:n], refs[n : 2 * n], refs[2 * n : 3 * n], refs[3 * n :]
    loads, stores = [], []
    for i in range(n):
        shape = ins[i].shape
        for j in range(PIECES if len(shape) == 3 else 1):
            k = len(loads)
            if len(shape) == 3:
                rows = shape[1] // PIECES
                at = (0, pl.ds(j * rows, rows))
            else:
                at = (slice(None),)
            loads.append(pltpu.make_async_copy(ins[i].at[at], bufs[i].at[at], sems.at[0, k]))
            stores.append(pltpu.make_async_copy(bufs[i].at[at], outs[i].at[at], sems.at[1, k]))
    for copy in loads:
        copy.start()
    for load, store in zip(loads, stores):
        load.wait()
        store.start()
    for copy in stores:
        copy.wait()


def per_device(tokens, cotangent, route, gates, w_gate, w_up, w_down):
    assert lax.axis_size("dp") == NZ * NX * NC and lax.axis_size("expert") == NS * NY
    feat = tokens.shape[1]
    hidden = w_gate.shape[1]
    rows = NC * NZ * ROWS
    dma = pltpu.SemaphoreType.DMA
    hbm = pl.BlockSpec(memory_space=pl.ANY)
    outs = (jax.ShapeDtypeStruct(tokens.shape, BF16),) * 2
    outs += (jax.ShapeDtypeStruct(w_gate.shape, BF16),) * 3
    nq = RING // QUAD
    results = pl.pallas_call(
        layer_kernel,
        out_shape=outs,
        in_specs=[hbm] * 7,
        out_specs=(hbm,) * 5,
        scratch_shapes=[
            pltpu.VMEM(tokens.shape, BF16),
            pltpu.VMEM(tokens.shape, BF16),
            pltpu.VMEM(route.shape[::-1], route.dtype),
            pltpu.VMEM(route.shape[::-1], gates.dtype),
            pltpu.VMEM(tokens.shape, BF16),
            pltpu.VMEM(tokens.shape, BF16),
            pltpu.VMEM((NY, NS * 2 * CAP, feat), F32),
            pltpu.VMEM((NX, NS * 2 * CAP, feat), F32),
            pltpu.VMEM((NS, 2, ROWS, feat), BF16),
            pltpu.VMEM((2, NX, NS, NC, NZ, ROWS, feat), BF16),
            pltpu.VMEM(w_gate.shape[1:], BF16),
            pltpu.VMEM(w_gate.shape[1:], BF16),
            pltpu.VMEM(w_gate.shape[1:], BF16),
            pltpu.VMEM((3, rows, hidden), BF16),
            pltpu.VMEM((2, NX, NS, NC, NZ, ROWS, feat), BF16),
            pltpu.VMEM((2, NX, NS, NZ, ROWS, feat), BF16),
            pltpu.VMEM((NX - 1, 2, NS, NZ, ROWS, feat), BF16),
            pltpu.VMEM((RING, 2, ROWS, feat), BF16),
            pltpu.VMEM((RING, 2, ROWS, feat), BF16),
            pltpu.VMEM((NX, NS * 2 * CAP, feat), F32),
            pltpu.VMEM((NY, NS * 2 * CAP, feat), F32),
            pltpu.VMEM(w_gate.shape[1:], BF16),
            pltpu.VMEM(w_gate.shape[1:], BF16),
            pltpu.VMEM(w_gate.shape[1:], BF16),
            dma((4,)),
            dma((3,)),
            dma((5,)),
            dma((96,)),
            dma((2, NY)),
            dma((RING,)),
            dma((NX - 1, 13)),
            dma((nq,)),
            dma((nq,)),
            dma((NX - 1, nq)),
            dma((RING,)),
            dma((2, NY)),
            pltpu.SemaphoreType.REGULAR,
        ],
        compiler_params=pltpu.CompilerParams(
            collective_id=0, has_side_effects=True, vmem_limit_bytes=62 << 20
        ),
        name="expert_layer",
    )(tokens, cotangent, route.T, gates.T, w_gate, w_up, w_down)
    return pl.pallas_call(
        functools.partial(store_kernel, len(outs)),
        out_shape=outs,
        in_specs=[hbm] * len(outs),
        out_specs=(hbm,) * len(outs),
        scratch_shapes=[pltpu.VMEM(out.shape, out.dtype) for out in outs] + [dma((2, 3 * PIECES + 2))],
        compiler_params=pltpu.CompilerParams(vmem_limit_bytes=62 << 20),
        name="store_results",
    )(*results)


def solution(mesh):
    return jax.shard_map(
        per_device,
        mesh=mesh,
        in_specs=(
            P("dp", "expert"),
            P("dp", "expert"),
            P("dp", None),
            P("dp", None),
            P("expert", "dp", None),
            P("expert", "dp", None),
            P("expert", "dp", None),
        ),
        out_specs=(
            P("dp", "expert"),
            P("dp", "expert"),
            P("expert", "dp", None),
            P("expert", "dp", None),
            P("expert", "dp", None),
        ),
        check_vma=False,
    )
```
